32 devices in a mesh: tm: 2 (over y), space: 16 (over z, x, core).
Axes of the slice: x: 2, y: 2, z: 4, core: 2. Of those that a mesh axis runs over, the one named last changes fastest.
Arguments:
- control: float32 [32, 51200], P(('tm', 'space')), may hold values from -4 to 4
- spectrum: float32 [51200], replicated, may hold values from 0.2 to 2
- perturb: bfloat16 [4, 32, 4, 51200], P('tm', None, None, 'space'), may hold values from -1 to 1
- obs_index: int32 [4, 32768], P('tm', 'space'), may hold values from 0 to 12799
- innovation: float32 [4, 32768], P('tm', 'space'), may hold values from -10 to 10
- obs_sigma: float32 [4, 32768], P('tm', 'space'), may hold values from 0.5 to 2
- qc_class: int32 [4, 32768], P('tm', 'space'), may hold values from 0 to 2
Outputs:
- control_out: float32 [32, 51200], P(('tm', 'space'))
- cost_list: float32 [1], replicated
The draws below stay inside these ranges and needn't reach their ends.
Inputs may be any that keep to these rules, and one draw needn't show every extreme that they name: `obs_index`: observation o of block o // 2048 observes the cell level * 3200 + point, the point counted within the block's piece of the grid; repeats may occur.
All inputs are finite; a program needn't handle non-finite values.
Results may differ from the reference program's by a relative error of at most 0.0034.
Values may be sent and summed in bfloat16 or wider, within the bound.
A program may use at most 128 MiB of HBM per device.

```python
import math
import jax
import jax.numpy as jnp
from jax import lax

GX = 320
GY = 160
LEV = 4
ITERS = 1
OBS_DEV = 2048
TIMES = 4
MEMBERS = 32
NOBS = 32768
N_SPACE = 16


def set_ends(entries, stream_key, smallest, top_value):
    longest = entries.shape.index(max(entries.shape))
    spots = []
    for shift in (0, 1):
        where = [jax.random.randint(jax.random.fold_in(stream_key, axis), (), 0, length) for axis, length in enumerate(entries.shape)]
        where[longest] = (where[longest] + shift) % entries.shape[longest]
        spots.append(tuple(where))
    return entries.at[spots[0]].set(smallest).at[spots[1]].set(top_value)


def shard_levels(own_key, dims, shards, low, high):
    def one(position, shards_of):
        draws = jax.random.uniform(jax.random.fold_in(jax.random.fold_in(own_key, 6), position), (shards_of,), jnp.float32, low / len(shards), high / len(shards))
        return jnp.repeat(jnp.exp(draws), dims[position] // shards_of).reshape((-1,) + (1,) * (len(dims) - position - 1))

    factor_of = one(*shards[0])
    for cut in shards[1:]:
        factor_of = factor_of * one(*cut)
    return factor_of


def noise(key, shape, spread, most, shards=(), held_as=jnp.bfloat16):
    drawn = spread * jax.random.normal(key, shape, jnp.float32)
    if shards:
        drawn = drawn * shard_levels(key, shape, shards, -0.22, 0.18)
    return jnp.clip(drawn, -most, most).astype(held_as)


def setup_inputs(seed: int = 0) -> dict:
    key_list = jax.random.split(jax.random.key(seed), 8)
    return {
        "control": noise(key_list[0], (MEMBERS, GX * GY), 0.5, 4.0, ((0, 32),), jnp.float32),
        "spectrum": jnp.clip(jnp.exp(jax.random.uniform(key_list[1], (GX * GY,), jnp.float32, math.log(0.2), math.log(2.0))), 0.2, 2.0),
        "perturb": noise(key_list[2], (TIMES, MEMBERS, LEV, GX * GY), MEMBERS ** -0.5, 1.0, ((0, 2), (3, 16))),
        "obs_index": set_ends(jax.random.randint(key_list[3], (TIMES, NOBS), 0, LEV * (GX * GY // N_SPACE)), jax.random.fold_in(key_list[3], 1), 0, (LEV * (GX * GY // N_SPACE)) - 1).astype(jnp.int32),
        "innovation": noise(key_list[4], (TIMES, NOBS), 2.0, 10.0, ((0, 2), (1, 16)), jnp.float32),
        "obs_sigma": jnp.clip(jnp.exp(math.log(2.0) - 1.3862944 * jax.random.uniform(key_list[5], (TIMES, NOBS), jnp.float32) ** shard_levels(key_list[5], (TIMES, NOBS), ((0, 2), (1, 16)), -0.2, 0.2)), 0.5, 2.0),
        "qc_class": set_ends(jax.random.randint(key_list[6], (TIMES, NOBS), 0, 3), jax.random.fold_in(key_list[6], 1), 0, 2).astype(jnp.int32),
    }


def lookup_tables(segment_length):
    wave_num = jnp.arange(segment_length, dtype=jnp.float32)[:, None]
    grid_positions = jnp.arange(segment_length, dtype=jnp.float32)[None, :]
    basis = jnp.cos(jnp.pi * (grid_positions + 0.5) * wave_num / segment_length) * jnp.sqrt(2.0 / segment_length)
    return jnp.where(wave_num == 0, basis * jnp.sqrt(0.5), basis)

def synthesize(control, spectrum, basis_x, basis_y):
    coeffs = (control * spectrum[None, :]).reshape(control.shape[0], GX, GY)
    middle = jnp.einsum('kn,mkl->mnl', basis_x, coeffs, precision=lax.Precision.HIGHEST)
    result = jnp.einsum('mnl,lp->mnp', middle, basis_y, precision=lax.Precision.HIGHEST)
    return result.reshape(control.shape[0], GX * GY)

def analyze(adjoint, spectrum, basis_x, basis_y):
    state_fields = adjoint.reshape(adjoint.shape[0], GX, GY)
    middle = jnp.einsum('kn,mnp->mkp', basis_x, state_fields, precision=lax.Precision.HIGHEST)
    result = jnp.einsum('mkp,lp->mkl', middle, basis_y, precision=lax.Precision.HIGHEST)
    return result.reshape(adjoint.shape[0], GX * GY) * spectrum[None, :]

def reference(control, spectrum, perturb, obs_index, innovation, obs_sigma, qc_class):
    basis_x = lookup_tables(GX)
    basis_y = lookup_tables(GY)
    grid_total = GX * GY
    piece_len = grid_total // N_SPACE
    block_ids = (jnp.arange(innovation.shape[1], dtype=jnp.int32) // OBS_DEV).astype(jnp.int32)
    cell_index = obs_index // piece_len * grid_total + block_ids[None, :] * piece_len + obs_index % piece_len
    cell_index = cell_index.astype(jnp.int32)
    radius = jnp.where(qc_class == 0, 4.0, jnp.where(qc_class == 1, 2.0, 1.0)).astype(jnp.float32)
    cost_list = []

    def scatter_cells(indices, values):
        return jnp.zeros((LEV * grid_total,), jnp.float32).at[indices].add(values)
    for iteration in range(ITERS):
        member_field = synthesize(control, spectrum, basis_x, basis_y).astype(jnp.bfloat16)
        field_wide = member_field.astype(jnp.float32)

        def forward(slot_data):
            return jnp.einsum('mlg,mg->lg', slot_data.astype(jnp.float32), field_wide).reshape(-1)
        increment = lax.map(forward, perturb)
        modelled = jnp.take_along_axis(increment, cell_index, axis=1)
        scaled = (modelled - innovation) / obs_sigma
        scaled_sq = scaled * scaled / (radius * radius)
        obs_cost = jnp.sum(0.5 * radius * radius * jnp.log1p(scaled_sq))
        back_cost = 0.5 * jnp.sum(control * control)
        obs_grad = scaled / ((1.0 + scaled_sq) * obs_sigma)
        control_update = jax.vmap(scatter_cells)(cell_index, obs_grad).astype(jnp.bfloat16)

        def backward(running, pair):
            slot_data, slot_update = pair
            term = jnp.einsum('mlg,lg->mg', slot_data.astype(jnp.float32), slot_update.reshape(LEV, grid_total).astype(jnp.float32))
            return (running + term, None)
        adjoint, unused = lax.scan(backward, jnp.zeros(control.shape, jnp.float32), (perturb, control_update))
        gradient = control + analyze(adjoint, spectrum, basis_x, basis_y)
        grad_sq = jnp.sum(gradient * gradient)
        total_cost = back_cost + obs_cost
        step_size = 0.5 * total_cost / (grad_sq + 1e-06)
        control = control - step_size * gradient
        cost_list.append(total_cost)
    return (control, jnp.stack(cost_list))
```

```python
import functools

import jax
import jax.numpy as jnp
import ml_dtypes
import numpy as np
from jax import lax
from jax.experimental import pallas as pl
from jax.experimental.pallas import tpu as pltpu
from jax.sharding import PartitionSpec as P

GX = 320
GY = 160


def lookup_tables(segment_length):
    wave_num = jnp.arange(segment_length, dtype=jnp.float32)[:, None]
    grid_positions = jnp.arange(segment_length, dtype=jnp.float32)[None, :]
    basis = jnp.cos(jnp.pi * (grid_positions + 0.5) * wave_num / segment_length) * jnp.sqrt(
        2.0 / segment_length
    )
    return jnp.where(wave_num == 0, basis * jnp.sqrt(0.5), basis)


def synthesize(control, spectrum, basis_x, basis_y):
    coeffs = (control * spectrum[None, :]).reshape(control.shape[0], GX, GY)
    middle = jnp.einsum("kn,mkl->mnl", basis_x, coeffs, precision=lax.Precision.HIGHEST)
    result = jnp.einsum("mnl,lp->mnp", middle, basis_y, precision=lax.Precision.HIGHEST)
    return result.reshape(control.shape[0], GX * GY)


def analyze(adjoint, spectrum, basis_x, basis_y):
    state_fields = adjoint.reshape(adjoint.shape[0], GX, GY)
    middle = jnp.einsum("kn,mnp->mkp", basis_x, state_fields, precision=lax.Precision.HIGHEST)
    result = jnp.einsum("mkp,lp->mkl", middle, basis_y, precision=lax.Precision.HIGHEST)
    return result.reshape(adjoint.shape[0], GX * GY) * spectrum[None, :]


def per_device(control, spectrum, perturb, obs_index, innovation, obs_sigma, qc_class):
    basis_x = lookup_tables(GX)
    basis_y = lookup_tables(GY)
    slot_count = perturb.shape[0]
    levels = perturb.shape[2]
    piece_len = perturb.shape[3]
    radius = jnp.where(qc_class == 0, 4.0, jnp.where(qc_class == 1, 2.0, 1.0)).astype(jnp.float32)

    def scatter_cells(indices, values):
        return jnp.zeros((levels * piece_len,), jnp.float32).at[indices].add(values)

    member_field = synthesize(control, spectrum, basis_x, basis_y).astype(jnp.bfloat16)
    pieces = lax.all_to_all(member_field, "space", split_axis=1, concat_axis=0, tiled=True)
    selected_entries = perturb
    increment = jnp.einsum(
        "dzab,zb->dab",
        selected_entries,
        lax.all_gather(pieces, "tm", axis=0, tiled=True),
        preferred_element_type=jnp.float32,
    )
    cells_flat = increment.reshape(slot_count, levels * piece_len)
    modelled = jnp.take_along_axis(cells_flat, obs_index, axis=1)
    scaled = (modelled - innovation) / obs_sigma
    scaled_sq = scaled * scaled / (radius * radius)
    obs_part = jnp.sum(0.5 * radius * radius * jnp.log1p(scaled_sq))
    back_part = 0.5 * jnp.sum(control * control)
    obs_grad = scaled / ((1.0 + scaled_sq) * obs_sigma)
    control_update = jax.vmap(scatter_cells)(obs_index, obs_grad).astype(jnp.bfloat16)
    control_update = control_update.reshape(slot_count, levels, piece_len)
    selected_entries = perturb
    summed_rows = lax.psum_scatter(
        jnp.einsum(
            "qiyr,qyr->ir", selected_entries, control_update, preferred_element_type=jnp.float32
        ).astype(jnp.bfloat16),
        "tm",
        scatter_dimension=0,
        tiled=True,
    ).astype(jnp.float32)
    adjoint = lax.all_to_all(
        summed_rows.astype(jnp.bfloat16), "space", split_axis=0, concat_axis=1, tiled=True
    ).astype(summed_rows.dtype)
    gradient = control + analyze(adjoint, spectrum, basis_x, basis_y)
    grad_part = jnp.sum(gradient * gradient)
    obs_cost, back_cost = lax.psum((obs_part, back_part), ("tm", "space"))
    grad_sq = lax.psum(grad_part, ("tm", "space"))
    total_cost = back_cost + obs_cost
    step_size = 0.5 * total_cost / (grad_sq + 1e-06)
    control = control - step_size * gradient
    cost_list = [total_cost]
    return (control, jnp.stack(cost_list))


LANES = 128
FOLD = 4
MESH_ID = pl.DeviceIdType.MESH
F32 = jnp.float32
BF16 = jnp.bfloat16


def basis64(n):
    k = np.arange(n, dtype=np.float64)[:, None]
    x = np.arange(n, dtype=np.float64)[None, :]
    c = np.sqrt(2.0 / n) * np.cos(np.pi * (x + 0.5) * k / n)
    c[0] *= np.sqrt(0.5)
    return c.astype(np.float32)


def two_parts(c):
    hi = c.astype(ml_dtypes.bfloat16)
    lo = (c - hi.astype(np.float32)).astype(ml_dtypes.bfloat16)
    return np.stack([hi, lo])


def folded_bases():
    cx, cy = basis64(GX), basis64(GY)
    order = np.arange(GX).reshape(GX // FOLD, FOLD).T.reshape(-1)
    cxp = cx[order][:, order]
    return [two_parts(np.ascontiguousarray(a)) for a in (cxp, cxp.T, cy, cy.T)]


def split2(x):
    hi = x.astype(BF16)
    return hi, (x - hi.astype(F32)).astype(BF16)


def split3(x):
    a = x.astype(BF16).astype(F32)
    b = (x - a).astype(BF16).astype(F32)
    return a, b, x - a - b


def mm(a, b):
    return jnp.dot(a, b, preferred_element_type=F32)


def dot_right(x, c_ref):
    hi, lo = split2(x)
    return mm(hi, c_ref[0]) + (mm(lo, c_ref[0]) + mm(hi, c_ref[1]))


def dot_left(c_ref, x):
    hi, lo = split2(x)
    return mm(c_ref[0], hi) + (mm(c_ref[0], lo) + mm(c_ref[1], hi))


def unfold(wide):
    return jnp.concatenate([wide[:, r * GY : (r + 1) * GY] for r in range(FOLD)], axis=0)


def fold(tall):
    q = GX // FOLD
    return jnp.concatenate([tall[r * q : (r + 1) * q] for r in range(FOLD)], axis=1)


def xor_of(bits, k):
    return sum(lax.rem(b + lax.rem(lax.div(k, 1 << i), 2), 2) * (1 << i) for i, b in enumerate(bits))


def gather_lanes(rows, lanes):
    return jnp.take_along_axis(rows, lanes, axis=1, mode="promise_in_bounds")


def step_kernel(nt, ns, n_in, *refs):
    sources, (out, cost_out), held = refs[:n_in], refs[n_in : n_in + 2], refs[n_in + 2 :]
    landed, in_sem, held = held[:n_in], held[n_in], held[n_in + 1 :]
    control, spectrum, cy, cxpt, index, perturb, innov, sigma, qc, cxp, cyt = landed
    (
    flat, send_f, recv_f, spread, table, hi_hot, lo_hot, upd, prod,
    send_a, recv_a, part, parts, sf_sem, rf_sem, sa_sem, ra_sem, sp_sem, rp_sem,
    ) = held
    n = nt * ns
    my_t, my_s = lax.axis_index("tm"), lax.axis_index("space")
    me = my_t * ns + my_s
    slots, levels, piece = sources[5].shape[0], sources[5].shape[2], sources[5].shape[3]
    rows = piece // LANES
    cells = rows * levels
    sent = rows + rows % 2
    pad_rows = send_f.shape[1]
    q, width = GX // FOLD, FOLD * GY
    tiles = width // LANES
    chunks = index.shape[0] // slots
    group = 8
    bits = [lax.rem(lax.div(me, 1 << i), 2) for i in range(n.bit_length() - 1)]

    def device(peer):
        return (lax.div(peer, ns), lax.rem(peer, ns))

    def peer_of(k):
        return me + sum((1 - 2 * b) * (1 << i) for i, b in enumerate(bits) if k >> i & 1)

    def load(i):
        return pltpu.make_async_copy(sources[i], landed[i], in_sem.at[i])

    for i in (0, 1, 2, 3, 4):
        load(i).start()

    barrier = pltpu.get_barrier_semaphore()

    def greet(d, c):
        peer = lax.rem(me + d, n)
        pl.semaphore_signal(barrier, inc=1, device_id=device(peer), device_id_type=MESH_ID)
        return c

    lax.fori_loop(1, n, greet, 0)

    def wide_of(ref):
        return jnp.concatenate(
            [ref[pl.ds(a, q, stride=tiles), :] for a in range(tiles)], axis=1
        )

    def flat_from(wide):
        for a in range(tiles):
            flat[pl.ds(a, q, stride=tiles), :] = wide[:, a * LANES : (a + 1) * LANES]

    for i in (0, 1, 2):
        load(i).wait()
    ctl = wide_of(control)
    spec = wide_of(spectrum)
    mid = dot_right(unfold(ctl * spec), cy)
    load(3).wait()
    flat_from(fold(dot_left(cxpt, mid)))
    flat[q * tiles :, :] = jnp.zeros((flat.shape[0] - q * tiles, LANES), F32)
    for s in range(ns):
        send_f[s] = flat[s * rows : s * rows + pad_rows, :].astype(BF16)

    pl.semaphore_wait(barrier, n - 1)

    def f_copy(k):
        peer = peer_of(k)
        t, s = device(peer)
        return pltpu.make_async_remote_copy(
            send_f.at[s, pl.ds(0, sent)], recv_f.at[me, pl.ds(0, sent)],
            sf_sem, rf_sem.at[k // group], device_id=(t, s), device_id_type=MESH_ID,
        )

    for k in range(n - 1, 0, -1):
        f_copy(k).start()
    recv_f[me] = send_f[my_s]

    for j in range(rows):
        pltpu.make_async_copy(
            sources[5].at[:, :, :, pl.ds(j * LANES, LANES)],
            perturb.at[:, :, pl.ds(j * levels, levels), :], in_sem.at[5],
        ).start()
    for i in range(6, n_in):
        load(i).start()

    back = 0.5 * jnp.sum(ctl * ctl, axis=0, keepdims=True)
    back = sum(back[:, a * LANES : (a + 1) * LANES] for a in range(tiles))
    table[...] = jnp.zeros(table.shape, F32)
    send_a[...] = jnp.zeros(send_a.shape, BF16)
    load(4).wait()
    hi_rows, lo_cols = hi_hot.shape[1], lo_hot.shape[2]
    his, los = [], []
    for t in range(slots):
        ix = index[pl.ds(t, chunks, stride=slots), :]
        level, point = ix // piece, ix % piece
        hi, lo = (point // LANES) * levels + level, point % LANES
        his.append(hi)
        los.append(lo)
        row = (hi // 16) * 8 + hi % 8
        col = (((hi // 8) % 2) * LANES + lo).T
        for c in range(chunks):
            at = pl.ds(c * LANES, LANES)
            hi_hot[t, :, at] = jnp.where(
                lax.broadcasted_iota(jnp.int32, (hi_rows, LANES), 0) == row[c : c + 1, :], 1.0, 0.0
            ).astype(BF16)
            lo_hot[t, at, :] = jnp.where(
                lax.broadcasted_iota(jnp.int32, (LANES, lo_cols), 1) == col[:, c : c + 1], 1.0, 0.0
            ).astype(BF16)
    whole = perturb.at[:, :, pl.ds(0, cells), :]
    pltpu.make_async_copy(whole, whole, in_sem.at[5]).wait()

    my_block = lax.div(me, group)
    block_bits = bits[group.bit_length() - 1 :]

    def add_group(g, own):
        block = xor_of(block_bits, g)
        arrived = recv_f.at[pl.ds(0, group - own), pl.ds(0, sent)]
        pltpu.make_async_copy(arrived, arrived, rf_sem.at[g]).wait()
        for i in range(group):
            f = recv_f[block * group + i].astype(F32)[:rows]
            for l in range(levels):
                spread[i, pl.ds(l, rows, stride=levels), :] = f
        for t in range(slots):
            total = table[t, pl.ds(0, cells), :]
            for i in range(group):
                p = perturb[t, block * group + i, pl.ds(0, cells), :].astype(F32)
                total = total + p * spread[i, pl.ds(0, cells), :]
            table[t, pl.ds(0, cells), :] = total

    add_group(0, 1)
    n_groups = n // group

    def next_group(i, c):
        g = lax.rem(2 * i, n_groups) + lax.div(2 * i, n_groups)
        add_group(g, 0)
        return c

    lax.fori_loop(1, n_groups, next_group, 0)

    for i in (6, 7, 8):
        load(i).wait()
    costs = []
    for t in range(slots):
        model = jnp.zeros((chunks, LANES), F32)
        for h in range(cells):
            picked = gather_lanes(jnp.broadcast_to(table[t, h : h + 1, :], (chunks, LANES)), los[t])
            model = jnp.where(his[t] == h, picked, model)
        mine = pl.ds(t, chunks, stride=slots)
        sg = sigma[mine, :]
        qct = qc[mine, :]
        rad = jnp.where(qct == 0, 4.0, jnp.where(qct == 1, 2.0, 1.0)).astype(F32)
        scaled = (model - innov[mine, :]) / sg
        sq = scaled * scaled / (rad * rad)
        costs.append((rad, sq))
        g = scaled / ((1.0 + sq) * sg)
        terms = jnp.concatenate(
            [
                hi_hot[t, :, c * LANES : (c + 1) * LANES]
                * jnp.broadcast_to(g[c : c + 1, :], (hi_rows, LANES)).astype(BF16)
                for c in range(chunks)
            ],
            axis=1,
        )
        u = mm(terms, lo_hot[t]).astype(BF16).astype(F32)
        for b in range(upd.shape[1] // 8):
            upd[t, b * 8 : (b + 1) * 8, :] = u[
                (b // 2) * 8 : (b // 2 + 1) * 8, (b % 2) * LANES : (b % 2 + 1) * LANES
            ]

    def a_copy(peer):
        return pltpu.make_async_remote_copy(
            send_a.at[peer, pl.ds(0, sent)], recv_a.at[me, pl.ds(0, sent)], sa_sem, ra_sem,
            device_id=device(peer), device_id_type=MESH_ID,
        )

    def one_member(m, to):
        prod[pl.ds(0, cells), :] = sum(
            perturb[t, m, pl.ds(0, cells), :].astype(F32) * upd[t, pl.ds(0, cells), :]
            for t in range(slots)
        )
        to[pl.ds(0, rows), :] = sum(
            prod[pl.ds(l, rows, stride=levels), :] for l in range(levels)
        ).astype(BF16)

    def next_member(i, before):
        peer = xor_of(bits, n - 1 - i)
        one_member(peer, send_a.at[peer])
        a_copy(before).start()
        return peer

    first = peer_of(n - 1)
    one_member(first, send_a.at[first])
    last = lax.fori_loop(1, n - 1, next_member, first)
    one_member(me, recv_a.at[me])
    a_copy(last).start()

    cost_row = back
    for rad, sq in costs:
        cost_row = cost_row + jnp.sum(0.5 * rad * rad * jnp.log1p(sq), axis=0, keepdims=True)
    part[0:1, :] = cost_row
    for i in (9, 10):
        load(i).wait()

    others = recv_a.at[pl.ds(0, n - 1), pl.ds(0, sent)]
    pltpu.make_async_copy(others, others, ra_sem).wait()
    for s in range(ns):
        flat[s * rows : (s + 1) * rows, :] = sum(
            recv_a[t * ns + s].astype(F32)[:rows] for t in range(nt)
        )
    mid = dot_left(cxp, unfold(wide_of(flat)))
    gr = ctl + spec * fold(dot_right(mid, cyt))
    sq = jnp.sum(gr * gr, axis=0, keepdims=True)
    part[1:2, :] = sum(sq[:, a * LANES : (a + 1) * LANES] for a in range(tiles))

    def s_copy(k):
        peer = peer_of(k)
        return pltpu.make_async_remote_copy(
            part, parts.at[me], sp_sem, rp_sem, device_id=device(peer), device_id_type=MESH_ID,
        )

    for k in range(n - 1, 0, -1):
        s_copy(k).start()
    parts[me] = part[...]
    flat_from(gr)
    all_sent = send_a.at[pl.ds(0, n - 1), pl.ds(0, sent)]
    pltpu.make_async_copy(all_sent, all_sent, sf_sem).wait()
    pltpu.make_async_copy(all_sent, all_sent, sa_sem).wait()

    all_parts = parts.at[pl.ds(0, n - 1)]
    pltpu.make_async_copy(all_parts, all_parts, sp_sem).wait()
    pltpu.make_async_copy(all_parts, all_parts, rp_sem).wait()
    sums = jnp.sum(jnp.sum(parts[...], axis=0), axis=1, keepdims=True)
    total_cost, grad_sq = sums[0:1, :], sums[1:2, :]
    step = 0.5 * total_cost / (grad_sq + 1e-06)
    out[...] = control[...] - step * flat[: q * tiles, :]
    cost_out[...] = jnp.broadcast_to(total_cost, cost_out.shape)


def fused_device(nt, ns, control, spectrum, perturb, obs_index, innovation, obs_sigma, qc_class):
    n = nt * ns
    slots, members, levels, piece = perturb.shape
    grid_rows = GX * GY // LANES
    rows = piece // LANES
    cells = rows * levels
    pad_rows = -(-rows // 16) * 16
    pad_cells = -(-cells // 16) * 16
    hi_rows = -(-cells // 32) * 16
    obs = obs_index.shape[1]
    vm = pl.BlockSpec(memory_space=pltpu.VMEM)
    dma = pltpu.SemaphoreType.DMA
    cxp, cxpt, cy, cyt = [jnp.asarray(b) for b in folded_bases()]

    def by_chunk(x):
        return x.reshape(slots, obs // LANES, LANES).transpose(1, 0, 2).reshape(-1, LANES)

    sources = [
        control.reshape(grid_rows, LANES), spectrum.reshape(grid_rows, LANES), cy, cxpt,
        by_chunk(obs_index), perturb, by_chunk(innovation), by_chunk(obs_sigma),
        by_chunk(qc_class), cxp, cyt,
    ]
    lands = [pltpu.VMEM(a.shape, a.dtype) for a in sources]
    lands[5] = pltpu.VMEM((slots, members, pad_cells, LANES), BF16)
    out, cost = pl.pallas_call(
        functools.partial(step_kernel, nt, ns, len(sources)),
        out_shape=(
            jax.ShapeDtypeStruct((grid_rows, LANES), F32),
            jax.ShapeDtypeStruct((1, LANES), F32),
        ),
        in_specs=[pl.BlockSpec(memory_space=pltpu.HBM)] * len(sources),
        out_specs=(vm, vm),
        scratch_shapes=[
            *lands,
            dma((len(sources),)),
            pltpu.VMEM((grid_rows + 16, LANES), F32),
            pltpu.VMEM((ns, pad_rows, LANES), BF16),
            pltpu.VMEM((n, pad_rows, LANES), BF16),
            pltpu.VMEM((8, pad_cells, LANES), F32),
            pltpu.VMEM((slots, pad_cells, LANES), F32),
            pltpu.VMEM((slots, hi_rows, obs), BF16),
            pltpu.VMEM((slots, obs, 2 * LANES), BF16),
            pltpu.VMEM((slots, -(-cells // 8) * 8, LANES), F32),
            pltpu.VMEM((pad_cells, LANES), F32),
            pltpu.VMEM((n, pad_rows, LANES), BF16),
            pltpu.VMEM((n, pad_rows, LANES), BF16),
            pltpu.VMEM((2, LANES), F32),
            pltpu.VMEM((n, 2, LANES), F32),
            dma, dma((n // 8,)), dma, dma, dma, dma,
        ],
        compiler_params=pltpu.CompilerParams(
            collective_id=0, has_side_effects=True, vmem_limit_bytes=24 << 20
        ),
        name="envar_step",
    )(*[pltpu.with_memory_space_constraint(a, pltpu.HBM) for a in sources])
    return out.reshape(control.shape), cost[0, :1]


def fused_fits(nt, ns, control, perturb, innovation):
    n = nt * ns
    piece = GX * GY // ns
    return (
        nt == 2
        and ns == 16
        and control.shape[0] == n
        and perturb.shape[2] == 4
        and piece % LANES == 0
        and (FOLD * GY) % LANES == 0
        and (GX // FOLD) % 8 == 0
        and innovation.shape[1] // ns == 16 * LANES
    )


def solution(mesh):
    nt, ns = mesh.shape["tm"], mesh.shape["space"]

    def whole(control, spectrum, perturb, obs_index, innovation, obs_sigma, qc_class):
        fits = fused_fits(nt, ns, control, perturb, innovation)
        body = functools.partial(fused_device, nt, ns) if fits else per_device
        return on_mesh(mesh, body)(
            control, spectrum, perturb, obs_index, innovation, obs_sigma, qc_class
        )

    return whole


def on_mesh(mesh, body):
    in_specs = (
        P(("tm", "space"), None),
        P(),
        P("tm", None, None, "space"),
        P("tm", "space"),
        P("tm", "space"),
        P("tm", "space"),
        P("tm", "space"),
    )
    out_specs = (P(("tm", "space"), None), P())
    return jax.shard_map(
        body, mesh=mesh, in_specs=in_specs, out_specs=out_specs, check_vma=False
    )
```

```python
import functools

import jax
import jax.numpy as jnp
import ml_dtypes
import numpy as np
from jax import lax
from jax.experimental import pallas as pl
from jax.experimental.pallas import tpu as pltpu
from jax.sharding import PartitionSpec as P

GX = 320
GY = 160


def lookup_tables(segment_length):
    wave_num = jnp.arange(segment_length, dtype=jnp.float32)[:, None]
    grid_positions = jnp.arange(segment_length, dtype=jnp.float32)[None, :]
    basis = jnp.cos(jnp.pi * (grid_positions + 0.5) * wave_num / segment_length) * jnp.sqrt(
        2.0 / segment_length
    )
    return jnp.where(wave_num == 0, basis * jnp.sqrt(0.5), basis)


def synthesize(control, spectrum, basis_x, basis_y):
    coeffs = (control * spectrum[None, :]).reshape(control.shape[0], GX, GY)
    middle = jnp.einsum("kn,mkl->mnl", basis_x, coeffs, precision=lax.Precision.HIGHEST)
    result = jnp.einsum("mnl,lp->mnp", middle, basis_y, precision=lax.Precision.HIGHEST)
    return result.reshape(control.shape[0], GX * GY)


def analyze(adjoint, spectrum, basis_x, basis_y):
    state_fields = adjoint.reshape(adjoint.shape[0], GX, GY)
    middle = jnp.einsum("kn,mnp->mkp", basis_x, state_fields, precision=lax.Precision.HIGHEST)
    result = jnp.einsum("mkp,lp->mkl", middle, basis_y, precision=lax.Precision.HIGHEST)
    return result.reshape(adjoint.shape[0], GX * GY) * spectrum[None, :]


def per_device(control, spectrum, perturb, obs_index, innovation, obs_sigma, qc_class):
    basis_x = lookup_tables(GX)
    basis_y = lookup_tables(GY)
    slot_count = perturb.shape[0]
    levels = perturb.shape[2]
    piece_len = perturb.shape[3]
    radius = jnp.where(qc_class == 0, 4.0, jnp.where(qc_class == 1, 2.0, 1.0)).astype(jnp.float32)

    def scatter_cells(indices, values):
        return jnp.zeros((levels * piece_len,), jnp.float32).at[indices].add(values)

    member_field = synthesize(control, spectrum, basis_x, basis_y).astype(jnp.bfloat16)
    pieces = lax.all_to_all(member_field, "space", split_axis=1, concat_axis=0, tiled=True)
    selected_entries = perturb
    increment = jnp.einsum(
        "dzab,zb->dab",
        selected_entries,
        lax.all_gather(pieces, "tm", axis=0, tiled=True),
        preferred_element_type=jnp.float32,
    )
    cells_flat = increment.reshape(slot_count, levels * piece_len)
    modelled = jnp.take_along_axis(cells_flat, obs_index, axis=1)
    scaled = (modelled - innovation) / obs_sigma
    scaled_sq = scaled * scaled / (radius * radius)
    obs_part = jnp.sum(0.5 * radius * radius * jnp.log1p(scaled_sq))
    back_part = 0.5 * jnp.sum(control * control)
    obs_grad = scaled / ((1.0 + scaled_sq) * obs_sigma)
    control_update = jax.vmap(scatter_cells)(obs_index, obs_grad).astype(jnp.bfloat16)
    control_update = control_update.reshape(slot_count, levels, piece_len)
    selected_entries = perturb
    summed_rows = lax.psum_scatter(
        jnp.einsum(
            "qiyr,qyr->ir", selected_entries, control_update, preferred_element_type=jnp.float32
        ).astype(jnp.bfloat16),
        "tm",
        scatter_dimension=0,
        tiled=True,
    ).astype(jnp.float32)
    adjoint = lax.all_to_all(
        summed_rows.astype(jnp.bfloat16), "space", split_axis=0, concat_axis=1, tiled=True
    ).astype(summed_rows.dtype)
    gradient = control + analyze(adjoint, spectrum, basis_x, basis_y)
    grad_part = jnp.sum(gradient * gradient)
    obs_cost, back_cost = lax.psum((obs_part, back_part), ("tm", "space"))
    grad_sq = lax.psum(grad_part, ("tm", "space"))
    total_cost = back_cost + obs_cost
    step_size = 0.5 * total_cost / (grad_sq + 1e-06)
    control = control - step_size * gradient
    cost_list = [total_cost]
    return (control, jnp.stack(cost_list))


LANES = 128
FOLD = 4
MESH_ID = pl.DeviceIdType.MESH
F32 = jnp.float32
BF16 = jnp.bfloat16


def basis64(n):
    k = np.arange(n, dtype=np.float64)[:, None]
    x = np.arange(n, dtype=np.float64)[None, :]
    c = np.sqrt(2.0 / n) * np.cos(np.pi * (x + 0.5) * k / n)
    c[0] *= np.sqrt(0.5)
    return c.astype(np.float32)


def folded_bases():
    cx, cy = basis64(GX), basis64(GY)
    order = np.arange(GX).reshape(GX // FOLD, FOLD).T.reshape(-1)
    cxp = cx[order][:, order]
    return [np.ascontiguousarray(a).astype(ml_dtypes.bfloat16) for a in (cxp, cxp.T, cy, cy.T)]


def mm(a, b):
    return jnp.dot(a, b, preferred_element_type=F32)


def unfold(wide):
    return jnp.concatenate([wide[:, r * GY : (r + 1) * GY] for r in range(FOLD)], axis=0)


def fold(tall):
    q = GX // FOLD
    return jnp.concatenate([tall[r * q : (r + 1) * q] for r in range(FOLD)], axis=1)


def xor_of(bits, k):
    return sum(lax.rem(b + lax.rem(lax.div(k, 1 << i), 2), 2) * (1 << i) for i, b in enumerate(bits))


def gather_lanes(rows, lanes):
    return jnp.take_along_axis(rows, lanes, axis=1, mode="promise_in_bounds")


def step_kernel(nt, ns, n_in, *refs):
    sources, (out, cost_out), held = refs[:n_in], refs[n_in : n_in + 2], refs[n_in + 2 :]
    landed, in_sem, held = held[:n_in], held[n_in], held[n_in + 1 :]
    control, spectrum, cy, cxpt, index, perturb, innov, sigma, qc, cxp, cyt = landed
    (
    flat, send_f, recv_f, spread, table, hi_hot, lo_hot, upd, prod,
    send_a, recv_a, part, parts, sf_sem, rf_sem, sa_sem, ra_sem, sp_sem, rp_sem,
    ) = held
    n = nt * ns
    my_t, my_s = lax.axis_index("tm"), lax.axis_index("space")
    me = my_t * ns + my_s
    slots, levels, piece = sources[5].shape[0], sources[5].shape[2], sources[5].shape[3]
    rows = piece // LANES
    cells = rows * levels
    sent = rows + rows % 2
    pad_rows = send_f.shape[1]
    q, width = GX // FOLD, FOLD * GY
    tiles = width // LANES
    chunks = index.shape[0] // slots
    group = 8
    bits = [lax.rem(lax.div(me, 1 << i), 2) for i in range(n.bit_length() - 1)]

    def device(peer):
        return (lax.div(peer, ns), lax.rem(peer, ns))

    def peer_of(k):
        return me + sum((1 - 2 * b) * (1 << i) for i, b in enumerate(bits) if k >> i & 1)

    def load(i):
        return pltpu.make_async_copy(sources[i], landed[i], in_sem.at[i])

    for i in (0, 1, 2, 3, 4):
        load(i).start()

    barrier = pltpu.get_barrier_semaphore()

    for k in range(n - 1, 0, -1):
        pl.semaphore_signal(
            barrier, inc=1, device_id=device(peer_of(k)), device_id_type=MESH_ID
        )

    def wide_of(ref):
        return jnp.concatenate(
            [ref[pl.ds(a, q, stride=tiles), :] for a in range(tiles)], axis=1
        )

    def flat_from(wide):
        for a in range(tiles):
            flat[pl.ds(a, q, stride=tiles), :] = wide[:, a * LANES : (a + 1) * LANES]

    for i in (0, 1, 2):
        load(i).wait()
    ctl = wide_of(control)
    spec = wide_of(spectrum)
    mid = mm(unfold((ctl * spec).astype(BF16)), cy[...]).astype(BF16)
    load(3).wait()
    flat_from(fold(mm(cxpt[...], mid)))
    flat[q * tiles :, :] = jnp.zeros((flat.shape[0] - q * tiles, LANES), F32)
    for s in range(ns):
        send_f[s] = flat[s * rows : s * rows + pad_rows, :].astype(BF16)

    pl.semaphore_wait(barrier, n - 1)

    def f_copy(k):
        peer = peer_of(k)
        t, s = device(peer)
        return pltpu.make_async_remote_copy(
            send_f.at[s, pl.ds(0, sent)], recv_f.at[me, pl.ds(0, sent)],
            sf_sem, rf_sem.at[k // group], device_id=(t, s), device_id_type=MESH_ID,
        )

    for k in range(n - 1, 0, -1):
        f_copy(k).start()
    recv_f[me] = send_f[my_s]

    for j in range(rows):
        pltpu.make_async_copy(
            sources[5].at[:, :, :, pl.ds(j * LANES, LANES)],
            perturb.at[:, :, pl.ds(j * levels, levels), :], in_sem.at[5],
        ).start()
    for i in range(6, n_in):
        load(i).start()

    back = 0.5 * jnp.sum(ctl * ctl, axis=0, keepdims=True)
    back = sum(back[:, a * LANES : (a + 1) * LANES] for a in range(tiles))
    table[...] = jnp.zeros(table.shape, F32)
    send_a[...] = jnp.zeros(send_a.shape, BF16)
    load(4).wait()
    hi_rows, lo_cols = hi_hot.shape[1], lo_hot.shape[2]
    his, los = [], []
    for t in range(slots):
        ix = index[pl.ds(t, chunks, stride=slots), :]
        level, point = ix // piece, ix % piece
        hi, lo = (point // LANES) * levels + level, point % LANES
        his.append(hi)
        los.append(lo)
        row = (hi // 16) * 8 + hi % 8
        col = (((hi // 8) % 2) * LANES + lo).T
        for c in range(chunks):
            at = pl.ds(c * LANES, LANES)
            hi_hot[t, :, at] = jnp.where(
                lax.broadcasted_iota(jnp.int32, (hi_rows, LANES), 0) == row[c : c + 1, :], 1.0, 0.0
            ).astype(BF16)
            lo_hot[t, at, :] = jnp.where(
                lax.broadcasted_iota(jnp.int32, (LANES, lo_cols), 1) == col[:, c : c + 1], 1.0, 0.0
            ).astype(BF16)
    whole = perturb.at[:, :, pl.ds(0, cells), :]
    pltpu.make_async_copy(whole, whole, in_sem.at[5]).wait()

    my_block = lax.div(me, group)
    block_bits = bits[group.bit_length() - 1 :]

    def add_group(g, own):
        block = xor_of(block_bits, g)
        arrived = recv_f.at[pl.ds(0, group - own), pl.ds(0, sent)]
        pltpu.make_async_copy(arrived, arrived, rf_sem.at[g]).wait()
        for i in range(group):
            f = recv_f[block * group + i].astype(F32)[:rows]
            for l in range(levels):
                spread[i, pl.ds(l, rows, stride=levels), :] = f
        for t in range(slots):
            total = table[t, pl.ds(0, cells), :]
            for i in range(group):
                p = perturb[t, block * group + i, pl.ds(0, cells), :].astype(F32)
                total = total + p * spread[i, pl.ds(0, cells), :]
            table[t, pl.ds(0, cells), :] = total

    add_group(0, 1)
    n_groups = n // group

    def next_group(i, c):
        g = lax.rem(2 * i, n_groups) + lax.div(2 * i, n_groups)
        add_group(g, 0)
        return c

    lax.fori_loop(1, n_groups, next_group, 0)

    for i in (6, 7, 8):
        load(i).wait()
    costs = []
    for t in range(slots):
        model = jnp.zeros((chunks, LANES), F32)
        for h in range(cells):
            picked = gather_lanes(jnp.broadcast_to(table[t, h : h + 1, :], (chunks, LANES)), los[t])
            model = jnp.where(his[t] == h, picked, model)
        mine = pl.ds(t, chunks, stride=slots)
        sg = sigma[mine, :]
        qct = qc[mine, :]
        rad = jnp.where(qct == 0, 4.0, jnp.where(qct == 1, 2.0, 1.0)).astype(F32)
        scaled = (model - innov[mine, :]) / sg
        sq = scaled * scaled / (rad * rad)
        costs.append((rad, sq))
        g = scaled / ((1.0 + sq) * sg)
        terms = jnp.concatenate(
            [
                hi_hot[t, :, c * LANES : (c + 1) * LANES]
                * jnp.broadcast_to(g[c : c + 1, :], (hi_rows, LANES)).astype(BF16)
                for c in range(chunks)
            ],
            axis=1,
        )
        u = mm(terms, lo_hot[t]).astype(BF16).astype(F32)
        for b in range(upd.shape[1] // 8):
            upd[t, b * 8 : (b + 1) * 8, :] = u[
                (b // 2) * 8 : (b // 2 + 1) * 8, (b % 2) * LANES : (b % 2 + 1) * LANES
            ]

    def a_copy(peer):
        return pltpu.make_async_remote_copy(
            send_a.at[peer, pl.ds(0, sent)], recv_a.at[me, pl.ds(0, sent)], sa_sem, ra_sem,
            device_id=device(peer), device_id_type=MESH_ID,
        )

    def one_member(m, to):
        prod[pl.ds(0, cells), :] = sum(
            perturb[t, m, pl.ds(0, cells), :].astype(F32) * upd[t, pl.ds(0, cells), :]
            for t in range(slots)
        )
        to[pl.ds(0, rows), :] = sum(
            prod[pl.ds(l, rows, stride=levels), :] for l in range(levels)
        ).astype(BF16)

    def next_member(i, before):
        peer = xor_of(bits, n - 1 - i)
        one_member(peer, send_a.at[peer])
        a_copy(before).start()
        return peer

    first = peer_of(n - 1)
    one_member(first, send_a.at[first])
    last = lax.fori_loop(1, n - 1, next_member, first)
    one_member(me, recv_a.at[me])
    a_copy(last).start()

    cost_row = back
    for rad, sq in costs:
        cost_row = cost_row + jnp.sum(0.5 * rad * rad * jnp.log1p(sq), axis=0, keepdims=True)
    part[0:1, :] = cost_row
    for i in (9, 10):
        load(i).wait()

    others = recv_a.at[pl.ds(0, n - 1), pl.ds(0, sent)]
    pltpu.make_async_copy(others, others, ra_sem).wait()
    for s in range(ns):
        flat[s * rows : (s + 1) * rows, :] = sum(
            recv_a[t * ns + s].astype(F32)[:rows] for t in range(nt)
        )
    mid = mm(cxp[...], unfold(wide_of(flat).astype(BF16))).astype(BF16)
    gr = ctl + spec * fold(mm(mid, cyt[...]))
    sq = jnp.sum(gr * gr, axis=0, keepdims=True)
    part[1:2, :] = sum(sq[:, a * LANES : (a + 1) * LANES] for a in range(tiles))

    def s_copy(k):
        peer = peer_of(k)
        return pltpu.make_async_remote_copy(
            part, parts.at[me], sp_sem, rp_sem, device_id=device(peer), device_id_type=MESH_ID,
        )

    for k in range(n - 1, 0, -1):
        s_copy(k).start()
    parts[me] = part[...]
    flat_from(gr)
    all_sent = send_a.at[pl.ds(0, n - 1), pl.ds(0, sent)]
    pltpu.make_async_copy(all_sent, all_sent, sf_sem).wait()
    pltpu.make_async_copy(all_sent, all_sent, sa_sem).wait()

    all_parts = parts.at[pl.ds(0, n - 1)]
    pltpu.make_async_copy(all_parts, all_parts, sp_sem).wait()
    pltpu.make_async_copy(all_parts, all_parts, rp_sem).wait()
    sums = jnp.sum(jnp.sum(parts[...], axis=0), axis=1, keepdims=True)
    total_cost, grad_sq = sums[0:1, :], sums[1:2, :]
    step = 0.5 * total_cost / (grad_sq + 1e-06)
    out[...] = control[...] - step * flat[: q * tiles, :]
    cost_out[...] = jnp.broadcast_to(total_cost, cost_out.shape)


def put_kernel(out, cost, out_to, cost_to, sem):
    copies = [
        pltpu.make_async_copy(src, dst, sem.at[i])
        for i, (src, dst) in enumerate(((out, out_to), (cost, cost_to)))
    ]
    for copy in copies:
        copy.start()
    for copy in copies:
        copy.wait()


def fused_device(nt, ns, control, spectrum, perturb, obs_index, innovation, obs_sigma, qc_class):
    n = nt * ns
    slots, members, levels, piece = perturb.shape
    grid_rows = GX * GY // LANES
    rows = piece // LANES
    cells = rows * levels
    pad_rows = -(-rows // 16) * 16
    pad_cells = -(-cells // 16) * 16
    hi_rows = -(-cells // 32) * 16
    obs = obs_index.shape[1]
    vm = pl.BlockSpec(memory_space=pltpu.VMEM)
    dma = pltpu.SemaphoreType.DMA
    cxp, cxpt, cy, cyt = [jnp.asarray(b) for b in folded_bases()]

    def by_chunk(x):
        return x.reshape(slots, obs // LANES, LANES).transpose(1, 0, 2).reshape(-1, LANES)

    sources = [
        control.reshape(grid_rows, LANES), spectrum.reshape(grid_rows, LANES), cy, cxpt,
        by_chunk(obs_index), perturb, by_chunk(innovation), by_chunk(obs_sigma),
        by_chunk(qc_class), cxp, cyt,
    ]
    lands = [pltpu.VMEM(a.shape, a.dtype) for a in sources]
    lands[5] = pltpu.VMEM((slots, members, pad_cells, LANES), BF16)
    out, cost = pl.pallas_call(
        functools.partial(step_kernel, nt, ns, len(sources)),
        out_shape=(
            jax.ShapeDtypeStruct((grid_rows, LANES), F32),
            jax.ShapeDtypeStruct((1, LANES), F32),
        ),
        in_specs=[pl.BlockSpec(memory_space=pltpu.HBM)] * len(sources),
        out_specs=(vm, vm),
        scratch_shapes=[
            *lands,
            dma((len(sources),)),
            pltpu.VMEM((grid_rows + 16, LANES), F32),
            pltpu.VMEM((ns, pad_rows, LANES), BF16),
            pltpu.VMEM((n, pad_rows, LANES), BF16),
            pltpu.VMEM((8, pad_cells, LANES), F32),
            pltpu.VMEM((slots, pad_cells, LANES), F32),
            pltpu.VMEM((slots, hi_rows, obs), BF16),
            pltpu.VMEM((slots, obs, 2 * LANES), BF16),
            pltpu.VMEM((slots, -(-cells // 8) * 8, LANES), F32),
            pltpu.VMEM((pad_cells, LANES), F32),
            pltpu.VMEM((n, pad_rows, LANES), BF16),
            pltpu.VMEM((n, pad_rows, LANES), BF16),
            pltpu.VMEM((2, LANES), F32),
            pltpu.VMEM((n, 2, LANES), F32),
            dma, dma((n // 8,)), dma, dma, dma, dma,
        ],
        compiler_params=pltpu.CompilerParams(
            collective_id=0, has_side_effects=True, vmem_limit_bytes=24 << 20
        ),
        name="envar_step",
    )(*[pltpu.with_memory_space_constraint(a, pltpu.HBM) for a in sources])
    out, cost = pl.pallas_call(
        put_kernel,
        out_shape=(
            jax.ShapeDtypeStruct((grid_rows, LANES), F32),
            jax.ShapeDtypeStruct((1, LANES), F32),
        ),
        in_specs=[pl.BlockSpec(memory_space=pltpu.VMEM)] * 2,
        out_specs=[pl.BlockSpec(memory_space=pltpu.HBM)] * 2,
        scratch_shapes=[dma((2,))],
        name="put_results",
    )(*[pltpu.with_memory_space_constraint(a, pltpu.VMEM) for a in (out, cost)])
    return out.reshape(control.shape), cost[0, :1]


def fused_fits(nt, ns, control, perturb, innovation):
    n = nt * ns
    piece = GX * GY // ns
    return (
        nt == 2
        and ns == 16
        and control.shape[0] == n
        and perturb.shape[2] == 4
        and piece % LANES == 0
        and (FOLD * GY) % LANES == 0
        and (GX // FOLD) % 8 == 0
        and innovation.shape[1] // ns == 16 * LANES
    )


def solution(mesh):
    nt, ns = mesh.shape["tm"], mesh.shape["space"]

    def whole(control, spectrum, perturb, obs_index, innovation, obs_sigma, qc_class):
        fits = fused_fits(nt, ns, control, perturb, innovation)
        body = functools.partial(fused_device, nt, ns) if fits else per_device
        return on_mesh(mesh, body)(
            control, spectrum, perturb, obs_index, innovation, obs_sigma, qc_class
        )

    return whole


def on_mesh(mesh, body):
    in_specs = (
        P(("tm", "space"), None),
        P(),
        P("tm", None, None, "space"),
        P("tm", "space"),
        P("tm", "space"),
        P("tm", "space"),
        P("tm", "space"),
    )
    out_specs = (P(("tm", "space"), None), P())
    return jax.shard_map(
        body, mesh=mesh, in_specs=in_specs, out_specs=out_specs, check_vma=False
    )
```

```python
import functools

import jax
import jax.numpy as jnp
import ml_dtypes
import numpy as np
from jax import lax
from jax.experimental import pallas as pl
from jax.experimental.pallas import tpu as pltpu
from jax.sharding import PartitionSpec as P

GX = 320
GY = 160


def lookup_tables(segment_length):
    wave_num = jnp.arange(segment_length, dtype=jnp.float32)[:, None]
    grid_positions = jnp.arange(segment_length, dtype=jnp.float32)[None, :]
    basis = jnp.cos(jnp.pi * (grid_positions + 0.5) * wave_num / segment_length) * jnp.sqrt(
        2.0 / segment_length
    )
    return jnp.where(wave_num == 0, basis * jnp.sqrt(0.5), basis)


def synthesize(control, spectrum, basis_x, basis_y):
    coeffs = (control * spectrum[None, :]).reshape(control.shape[0], GX, GY)
    middle = jnp.einsum("kn,mkl->mnl", basis_x, coeffs, precision=lax.Precision.HIGHEST)
    result = jnp.einsum("mnl,lp->mnp", middle, basis_y, precision=lax.Precision.HIGHEST)
    return result.reshape(control.shape[0], GX * GY)


def analyze(adjoint, spectrum, basis_x, basis_y):
    state_fields = adjoint.reshape(adjoint.shape[0], GX, GY)
    middle = jnp.einsum("kn,mnp->mkp", basis_x, state_fields, precision=lax.Precision.HIGHEST)
    result = jnp.einsum("mkp,lp->mkl", middle, basis_y, precision=lax.Precision.HIGHEST)
    return result.reshape(adjoint.shape[0], GX * GY) * spectrum[None, :]


def per_device(control, spectrum, perturb, obs_index, innovation, obs_sigma, qc_class):
    basis_x = lookup_tables(GX)
    basis_y = lookup_tables(GY)
    slot_count = perturb.shape[0]
    levels = perturb.shape[2]
    piece_len = perturb.shape[3]
    radius = jnp.where(qc_class == 0, 4.0, jnp.where(qc_class == 1, 2.0, 1.0)).astype(jnp.float32)

    def scatter_cells(indices, values):
        return jnp.zeros((levels * piece_len,), jnp.float32).at[indices].add(values)

    member_field = synthesize(control, spectrum, basis_x, basis_y).astype(jnp.bfloat16)
    pieces = lax.all_to_all(member_field, "space", split_axis=1, concat_axis=0, tiled=True)
    selected_entries = perturb
    increment = jnp.einsum(
        "dzab,zb->dab",
        selected_entries,
        lax.all_gather(pieces, "tm", axis=0, tiled=True),
        preferred_element_type=jnp.float32,
    )
    cells_flat = increment.reshape(slot_count, levels * piece_len)
    modelled = jnp.take_along_axis(cells_flat, obs_index, axis=1)
    scaled = (modelled - innovation) / obs_sigma
    scaled_sq = scaled * scaled / (radius * radius)
    obs_part = jnp.sum(0.5 * radius * radius * jnp.log1p(scaled_sq))
    back_part = 0.5 * jnp.sum(control * control)
    obs_grad = scaled / ((1.0 + scaled_sq) * obs_sigma)
    control_update = jax.vmap(scatter_cells)(obs_index, obs_grad).astype(jnp.bfloat16)
    control_update = control_update.reshape(slot_count, levels, piece_len)
    selected_entries = perturb
    summed_rows = lax.psum_scatter(
        jnp.einsum(
            "qiyr,qyr->ir", selected_entries, control_update, preferred_element_type=jnp.float32
        ).astype(jnp.bfloat16),
        "tm",
        scatter_dimension=0,
        tiled=True,
    ).astype(jnp.float32)
    adjoint = lax.all_to_all(
        summed_rows.astype(jnp.bfloat16), "space", split_axis=0, concat_axis=1, tiled=True
    ).astype(summed_rows.dtype)
    gradient = control + analyze(adjoint, spectrum, basis_x, basis_y)
    grad_part = jnp.sum(gradient * gradient)
    obs_cost, back_cost = lax.psum((obs_part, back_part), ("tm", "space"))
    grad_sq = lax.psum(grad_part, ("tm", "space"))
    total_cost = back_cost + obs_cost
    step_size = 0.5 * total_cost / (grad_sq + 1e-06)
    control = control - step_size * gradient
    cost_list = [total_cost]
    return (control, jnp.stack(cost_list))


LANES = 128
FOLD = 4
MESH_ID = pl.DeviceIdType.MESH
F32 = jnp.float32
BF16 = jnp.bfloat16


def basis64(n):
    k = np.arange(n, dtype=np.float64)[:, None]
    x = np.arange(n, dtype=np.float64)[None, :]
    c = np.sqrt(2.0 / n) * np.cos(np.pi * (x + 0.5) * k / n)
    c[0] *= np.sqrt(0.5)
    return c.astype(np.float32)


def folded_bases():
    cx, cy = basis64(GX), basis64(GY)
    order = np.arange(GX).reshape(GX // FOLD, FOLD).T.reshape(-1)
    cxp = cx[order][:, order]
    return [np.ascontiguousarray(a).astype(ml_dtypes.bfloat16) for a in (cxp, cxp.T, cy, cy.T)]


def mm(a, b):
    return jnp.dot(a, b, preferred_element_type=F32)


def unfold(wide):
    return jnp.concatenate([wide[:, r * GY : (r + 1) * GY] for r in range(FOLD)], axis=0)


def fold(tall):
    q = GX // FOLD
    return jnp.concatenate([tall[r * q : (r + 1) * q] for r in range(FOLD)], axis=1)


def xor_of(bits, k):
    return sum(lax.rem(b + lax.rem(lax.div(k, 1 << i), 2), 2) * (1 << i) for i, b in enumerate(bits))


def gather_lanes(rows, lanes):
    return jnp.take_along_axis(rows, lanes, axis=1, mode="promise_in_bounds")


def step_kernel(nt, ns, n_in, *refs):
    sources, (out, cost_out), held = refs[:n_in], refs[n_in : n_in + 2], refs[n_in + 2 :]
    landed, in_sem, held = held[:n_in], held[n_in], held[n_in + 1 :]
    control, spectrum, cy, cxpt, index, perturb, innov, sigma, qc, cxp, cyt = landed
    (
    flat, send_f, recv_f, spread, table, hi_hot, lo_hot, upd, prod,
    send_a, recv_a, part, parts, sf_sem, rf_sem, sa_sem, ra_sem, sp_sem, rp_sem,
    ) = held
    n = nt * ns
    my_t, my_s = lax.axis_index("tm"), lax.axis_index("space")
    me = my_t * ns + my_s
    slots, levels, piece = sources[5].shape[0], sources[5].shape[2], sources[5].shape[3]
    rows = piece // LANES
    cells = rows * levels
    sent = rows + rows % 2
    pad_rows = send_f.shape[1]
    q, width = GX // FOLD, FOLD * GY
    tiles = width // LANES
    chunks = index.shape[0] // slots
    group = 8
    bits = [lax.rem(lax.div(me, 1 << i), 2) for i in range(n.bit_length() - 1)]
    n_groups = n // group
    ranges = [(16, rows - 16, sent - 16), (0, 16, 16)] if rows > 16 else [(0, rows, sent)]

    def device(peer):
        return (lax.div(peer, ns), lax.rem(peer, ns))

    def peer_of(k):
        return me + sum((1 - 2 * b) * (1 << i) for i, b in enumerate(bits) if k >> i & 1)

    def load(i):
        return pltpu.make_async_copy(sources[i], landed[i], in_sem.at[i])

    for i in (0, 1, 2, 3, 4):
        load(i).start()

    barrier = pltpu.get_barrier_semaphore()

    for k in range(n - 1, 0, -1):
        pl.semaphore_signal(
            barrier, inc=1, device_id=device(peer_of(k)), device_id_type=MESH_ID
        )

    def wide_of(ref):
        return jnp.concatenate(
            [ref[pl.ds(a, q, stride=tiles), :] for a in range(tiles)], axis=1
        )

    def flat_from(wide):
        for a in range(tiles):
            flat[pl.ds(a, q, stride=tiles), :] = wide[:, a * LANES : (a + 1) * LANES]

    for i in (0, 1, 2):
        load(i).wait()
    ctl = wide_of(control)
    spec = wide_of(spectrum)
    mid = mm(unfold((ctl * spec).astype(BF16)), cy[...]).astype(BF16)
    load(3).wait()
    flat_from(fold(mm(cxpt[...], mid)))
    flat[q * tiles :, :] = jnp.zeros((flat.shape[0] - q * tiles, LANES), F32)
    for s in range(ns):
        send_f[s] = flat[s * rows : s * rows + pad_rows, :].astype(BF16)

    pl.semaphore_wait(barrier, n - 1)

    def f_copy(p, k):
        peer = peer_of(k)
        t, s = device(peer)
        at = pl.ds(ranges[p][0], ranges[p][2])
        return pltpu.make_async_remote_copy(
            send_f.at[s, at], recv_f.at[me, at], sf_sem, rf_sem.at[p * n_groups + k // group],
            device_id=(t, s), device_id_type=MESH_ID,
        )

    for p in range(len(ranges)):
        for k in range(n - 1, 0, -1):
            f_copy(p, k).start()
    recv_f[me] = send_f[my_s]

    for j in range(rows):
        pltpu.make_async_copy(
            sources[5].at[:, :, :, pl.ds(j * LANES, LANES)],
            perturb.at[:, :, pl.ds(j * levels, levels), :], in_sem.at[5],
        ).start()
    for i in range(6, n_in):
        load(i).start()

    back = 0.5 * jnp.sum(ctl * ctl, axis=0, keepdims=True)
    back = sum(back[:, a * LANES : (a + 1) * LANES] for a in range(tiles))
    table[...] = jnp.zeros(table.shape, F32)
    send_a[...] = jnp.zeros(send_a.shape, BF16)
    load(4).wait()
    hi_rows, lo_cols = hi_hot.shape[1], lo_hot.shape[2]
    his, los = [], []
    for t in range(slots):
        ix = index[pl.ds(t, chunks, stride=slots), :]
        level, point = ix // piece, ix % piece
        hi, lo = (point // LANES) * levels + level, point % LANES
        his.append(hi)
        los.append(lo)
        col = lo.T
        for c in range(chunks):
            at = pl.ds(c * LANES, LANES)
            hi_hot[t, :, at] = jnp.where(
                lax.broadcasted_iota(jnp.int32, (hi_rows, LANES), 0) == hi[c : c + 1, :], 1.0, 0.0
            ).astype(BF16)
            lo_hot[t, at, :] = jnp.where(
                lax.broadcasted_iota(jnp.int32, (LANES, lo_cols), 1) == col[:, c : c + 1], 1.0, 0.0
            ).astype(BF16)
    whole = perturb.at[:, :, pl.ds(0, cells), :]
    pltpu.make_async_copy(whole, whole, in_sem.at[5]).wait()

    block_bits = bits[group.bit_length() - 1 :]

    def add_group(p, g, own):
        r0, real, wide = ranges[p]
        at = pl.ds(r0 * levels, real * levels)
        block = xor_of(block_bits, g)
        arrived = recv_f.at[pl.ds(0, group - own), pl.ds(0, wide)]
        pltpu.make_async_copy(arrived, arrived, rf_sem.at[p * n_groups + g]).wait()
        for i in range(group):
            f = recv_f[block * group + i, r0:, :].astype(F32)[:real]
            for l in range(levels):
                spread[i, pl.ds(r0 * levels + l, real, stride=levels), :] = f
        for t in range(slots):
            total = table[t, at, :]
            for i in range(group):
                v = perturb[t, block * group + i, at, :].astype(F32)
                total = total + v * spread[i, at, :]
            table[t, at, :] = total

    def increments(p):
        add_group(p, 0, 1)

        def next_group(i, c):
            g = lax.rem(2 * i, n_groups) + lax.div(2 * i, n_groups)
            add_group(p, g, 0)
            return c

        lax.fori_loop(1, n_groups, next_group, 0)

    models = [jnp.zeros((chunks, LANES), F32) for t in range(slots)]
    costs = [None] * slots

    def observe(p):
        r0, real, wide = ranges[p]
        top = hi_rows if r0 + real == rows else (r0 + real) * levels
        for t in range(slots):
            for h in range(r0 * levels, (r0 + real) * levels):
                picked = gather_lanes(
                    jnp.broadcast_to(table[t, h : h + 1, :], (chunks, LANES)), los[t]
                )
                models[t] = jnp.where(his[t] == h, picked, models[t])
            mine = pl.ds(t, chunks, stride=slots)
            sg = sigma[mine, :]
            qct = qc[mine, :]
            rad = jnp.where(qct == 0, 4.0, jnp.where(qct == 1, 2.0, 1.0)).astype(F32)
            scaled = (models[t] - innov[mine, :]) / sg
            sq = scaled * scaled / (rad * rad)
            costs[t] = (rad, sq)
            g = scaled / ((1.0 + sq) * sg)
            terms = jnp.concatenate(
                [
                    hi_hot[t, r0 * levels : top, c * LANES : (c + 1) * LANES]
                    * jnp.broadcast_to(g[c : c + 1, :], (top - r0 * levels, LANES)).astype(BF16)
                    for c in range(chunks)
                ],
                axis=1,
            )
            upd[t, r0 * levels : top, :] = mm(terms, lo_hot[t]).astype(BF16).astype(F32)

    def a_copy(p, peer):
        at = pl.ds(ranges[p][0], ranges[p][2])
        return pltpu.make_async_remote_copy(
            send_a.at[peer, at], recv_a.at[me, at], sa_sem, ra_sem,
            device_id=device(peer), device_id_type=MESH_ID,
        )

    def one_member(p, m, i, to):
        r0, real, wide = ranges[p]
        at = pl.ds(r0 * levels, real * levels)
        prod[i, at, :] = sum(
            perturb[t, m, at, :].astype(F32) * upd[t, at, :] for t in range(slots)
        )
        to[pl.ds(r0, real), :] = sum(
            prod[i, pl.ds(r0 * levels + l, real, stride=levels), :] for l in range(levels)
        ).astype(BF16)

    def low_of(i):
        return sum((1 - 2 * b) * (1 << j) for j, b in enumerate(bits[:3]) if i >> j & 1)

    def adjoints(p):
        def eight(d, before):
            base = xor_of(block_bits, n_groups - 1 - d) * group + lax.rem(me, group)
            for i in range(group - 1, -1, -1):
                peer = base + low_of(i)
                one_member(p, peer, i, send_a.at[peer])
                if i < group - 1:
                    a_copy(p, base + low_of(i + 1)).start()
            return base

        def next_eight(d, before):
            a_copy(p, before).start()
            return eight(d, before)

        last = lax.fori_loop(1, n_groups - 1, next_eight, eight(0, 0))
        for i in range(group - 1, 0, -1):
            peer = peer_of(i)
            one_member(p, peer, i, send_a.at[peer])
            a_copy(p, last if i == group - 1 else peer_of(i + 1)).start()
        one_member(p, me, 0, recv_a.at[me])
        a_copy(p, peer_of(1)).start()

    for p in range(len(ranges)):
        increments(p)
        if p == 0:
            for i in (6, 7, 8):
                load(i).wait()
        observe(p)
        adjoints(p)

    cost_row = back
    for rad, sq in costs:
        cost_row = cost_row + jnp.sum(0.5 * rad * rad * jnp.log1p(sq), axis=0, keepdims=True)
    part[0:1, :] = cost_row
    for i in (9, 10):
        load(i).wait()

    others = recv_a.at[pl.ds(0, n - 1), pl.ds(0, sent)]
    pltpu.make_async_copy(others, others, ra_sem).wait()
    for s in range(ns):
        flat[s * rows : (s + 1) * rows, :] = sum(
            recv_a[t * ns + s].astype(F32)[:rows] for t in range(nt)
        )
    mid = mm(cxp[...], unfold(wide_of(flat).astype(BF16))).astype(BF16)
    gr = ctl + spec * fold(mm(mid, cyt[...]))
    sq = jnp.sum(gr * gr, axis=0, keepdims=True)
    part[1:2, :] = sum(sq[:, a * LANES : (a + 1) * LANES] for a in range(tiles))

    def s_copy(k):
        peer = peer_of(k)
        return pltpu.make_async_remote_copy(
            part, parts.at[me], sp_sem, rp_sem, device_id=device(peer), device_id_type=MESH_ID,
        )

    for k in range(n - 1, 0, -1):
        s_copy(k).start()
    parts[me] = part[...]
    flat_from(gr)
    all_sent = send_a.at[pl.ds(0, n - 1), pl.ds(0, sent)]
    pltpu.make_async_copy(all_sent, all_sent, sf_sem).wait()
    pltpu.make_async_copy(all_sent, all_sent, sa_sem).wait()

    all_parts = parts.at[pl.ds(0, n - 1)]
    pltpu.make_async_copy(all_parts, all_parts, sp_sem).wait()
    pltpu.make_async_copy(all_parts, all_parts, rp_sem).wait()
    sums = jnp.sum(jnp.sum(parts[...], axis=0), axis=1, keepdims=True)
    total_cost, grad_sq = sums[0:1, :], sums[1:2, :]
    step = 0.5 * total_cost / (grad_sq + 1e-06)
    out[...] = control[...] - step * flat[: q * tiles, :]
    cost_out[...] = jnp.broadcast_to(total_cost, cost_out.shape)


def put_kernel(out, cost, out_to, cost_to, sem):
    copies = [
        pltpu.make_async_copy(src, dst, sem.at[i])
        for i, (src, dst) in enumerate(((out, out_to), (cost, cost_to)))
    ]
    for copy in copies:
        copy.start()
    for copy in copies:
        copy.wait()


def fused_device(nt, ns, control, spectrum, perturb, obs_index, innovation, obs_sigma, qc_class):
    n = nt * ns
    slots, members, levels, piece = perturb.shape
    grid_rows = GX * GY // LANES
    rows = piece // LANES
    cells = rows * levels
    pad_rows = -(-rows // 16) * 16
    pad_cells = -(-cells // 16) * 16
    hi_rows = pad_cells
    obs = obs_index.shape[1]
    vm = pl.BlockSpec(memory_space=pltpu.VMEM)
    dma = pltpu.SemaphoreType.DMA
    cxp, cxpt, cy, cyt = [jnp.asarray(b) for b in folded_bases()]

    def by_chunk(x):
        return x.reshape(slots, obs // LANES, LANES).transpose(1, 0, 2).reshape(-1, LANES)

    sources = [
        control.reshape(grid_rows, LANES), spectrum.reshape(grid_rows, LANES), cy, cxpt,
        by_chunk(obs_index), perturb, by_chunk(innovation), by_chunk(obs_sigma),
        by_chunk(qc_class), cxp, cyt,
    ]
    lands = [pltpu.VMEM(a.shape, a.dtype) for a in sources]
    lands[5] = pltpu.VMEM((slots, members, pad_cells, LANES), BF16)
    out, cost = pl.pallas_call(
        functools.partial(step_kernel, nt, ns, len(sources)),
        out_shape=(
            jax.ShapeDtypeStruct((grid_rows, LANES), F32),
            jax.ShapeDtypeStruct((1, LANES), F32),
        ),
        in_specs=[pl.BlockSpec(memory_space=pltpu.HBM)] * len(sources),
        out_specs=(vm, vm),
        scratch_shapes=[
            *lands,
            dma((len(sources),)),
            pltpu.VMEM((grid_rows + 16, LANES), F32),
            pltpu.VMEM((ns, pad_rows, LANES), BF16),
            pltpu.VMEM((n, pad_rows, LANES), BF16),
            pltpu.VMEM((8, pad_cells, LANES), F32),
            pltpu.VMEM((slots, pad_cells, LANES), F32),
            pltpu.VMEM((slots, hi_rows, obs), BF16),
            pltpu.VMEM((slots, obs, LANES), BF16),
            pltpu.VMEM((slots, pad_cells, LANES), F32),
            pltpu.VMEM((8, pad_cells, LANES), F32),
            pltpu.VMEM((n, pad_rows, LANES), BF16),
            pltpu.VMEM((n, pad_rows, LANES), BF16),
            pltpu.VMEM((2, LANES), F32),
            pltpu.VMEM((n, 2, LANES), F32),
            dma, dma((n // 4,)), dma, dma, dma, dma,
        ],
        compiler_params=pltpu.CompilerParams(
            collective_id=0, has_side_effects=True, vmem_limit_bytes=24 << 20
        ),
        name="envar_step",
    )(*[pltpu.with_memory_space_constraint(a, pltpu.HBM) for a in sources])
    out, cost = pl.pallas_call(
        put_kernel,
        out_shape=(
            jax.ShapeDtypeStruct((grid_rows, LANES), F32),
            jax.ShapeDtypeStruct((1, LANES), F32),
        ),
        in_specs=[pl.BlockSpec(memory_space=pltpu.VMEM)] * 2,
        out_specs=[pl.BlockSpec(memory_space=pltpu.HBM)] * 2,
        scratch_shapes=[dma((2,))],
        name="put_results",
    )(*[pltpu.with_memory_space_constraint(a, pltpu.VMEM) for a in (out, cost)])
    return out.reshape(control.shape), cost[0, :1]


def fused_fits(nt, ns, control, perturb, innovation):
    n = nt * ns
    piece = GX * GY // ns
    return (
        nt == 2
        and ns == 16
        and control.shape[0] == n
        and perturb.shape[2] == 4
        and piece % LANES == 0
        and (FOLD * GY) % LANES == 0
        and (GX // FOLD) % 8 == 0
        and innovation.shape[1] // ns == 16 * LANES
    )


def solution(mesh):
    nt, ns = mesh.shape["tm"], mesh.shape["space"]

    def whole(control, spectrum, perturb, obs_index, innovation, obs_sigma, qc_class):
        fits = fused_fits(nt, ns, control, perturb, innovation)
        body = functools.partial(fused_device, nt, ns) if fits else per_device
        return on_mesh(mesh, body)(
            control, spectrum, perturb, obs_index, innovation, obs_sigma, qc_class
        )

    return whole


def on_mesh(mesh, body):
    in_specs = (
        P(("tm", "space"), None),
        P(),
        P("tm", None, None, "space"),
        P("tm", "space"),
        P("tm", "space"),
        P("tm", "space"),
        P("tm", "space"),
    )
    out_specs = (P(("tm", "space"), None), P())
    return jax.shard_map(
        body, mesh=mesh, in_specs=in_specs, out_specs=out_specs, check_vma=False
    )
```

```python
import functools

import jax
import jax.numpy as jnp
import ml_dtypes
import numpy as np
from jax import lax
from jax.experimental import pallas as pl
from jax.experimental.pallas import tpu as pltpu
from jax.sharding import PartitionSpec as P

GX = 320
GY = 160


def lookup_tables(segment_length):
    wave_num = jnp.arange(segment_length, dtype=jnp.float32)[:, None]
    grid_positions = jnp.arange(segment_length, dtype=jnp.float32)[None, :]
    basis = jnp.cos(jnp.pi * (grid_positions + 0.5) * wave_num / segment_length) * jnp.sqrt(
        2.0 / segment_length
    )
    return jnp.where(wave_num == 0, basis * jnp.sqrt(0.5), basis)


def synthesize(control, spectrum, basis_x, basis_y):
    coeffs = (control * spectrum[None, :]).reshape(control.shape[0], GX, GY)
    middle = jnp.einsum("kn,mkl->mnl", basis_x, coeffs, precision=lax.Precision.HIGHEST)
    result = jnp.einsum("mnl,lp->mnp", middle, basis_y, precision=lax.Precision.HIGHEST)
    return result.reshape(control.shape[0], GX * GY)


def analyze(adjoint, spectrum, basis_x, basis_y):
    state_fields = adjoint.reshape(adjoint.shape[0], GX, GY)
    middle = jnp.einsum("kn,mnp->mkp", basis_x, state_fields, precision=lax.Precision.HIGHEST)
    result = jnp.einsum("mkp,lp->mkl", middle, basis_y, precision=lax.Precision.HIGHEST)
    return result.reshape(adjoint.shape[0], GX * GY) * spectrum[None, :]


def per_device(control, spectrum, perturb, obs_index, innovation, obs_sigma, qc_class):
    basis_x = lookup_tables(GX)
    basis_y = lookup_tables(GY)
    slot_count = perturb.shape[0]
    levels = perturb.shape[2]
    piece_len = perturb.shape[3]
    radius = jnp.where(qc_class == 0, 4.0, jnp.where(qc_class == 1, 2.0, 1.0)).astype(jnp.float32)

    def scatter_cells(indices, values):
        return jnp.zeros((levels * piece_len,), jnp.float32).at[indices].add(values)

    member_field = synthesize(control, spectrum, basis_x, basis_y).astype(jnp.bfloat16)
    pieces = lax.all_to_all(member_field, "space", split_axis=1, concat_axis=0, tiled=True)
    selected_entries = perturb
    increment = jnp.einsum(
        "dzab,zb->dab",
        selected_entries,
        lax.all_gather(pieces, "tm", axis=0, tiled=True),
        preferred_element_type=jnp.float32,
    )
    cells_flat = increment.reshape(slot_count, levels * piece_len)
    modelled = jnp.take_along_axis(cells_flat, obs_index, axis=1)
    scaled = (modelled - innovation) / obs_sigma
    scaled_sq = scaled * scaled / (radius * radius)
    obs_part = jnp.sum(0.5 * radius * radius * jnp.log1p(scaled_sq))
    back_part = 0.5 * jnp.sum(control * control)
    obs_grad = scaled / ((1.0 + scaled_sq) * obs_sigma)
    control_update = jax.vmap(scatter_cells)(obs_index, obs_grad).astype(jnp.bfloat16)
    control_update = control_update.reshape(slot_count, levels, piece_len)
    selected_entries = perturb
    summed_rows = lax.psum_scatter(
        jnp.einsum(
            "qiyr,qyr->ir", selected_entries, control_update, preferred_element_type=jnp.float32
        ).astype(jnp.bfloat16),
        "tm",
        scatter_dimension=0,
        tiled=True,
    ).astype(jnp.float32)
    adjoint = lax.all_to_all(
        summed_rows.astype(jnp.bfloat16), "space", split_axis=0, concat_axis=1, tiled=True
    ).astype(summed_rows.dtype)
    gradient = control + analyze(adjoint, spectrum, basis_x, basis_y)
    grad_part = jnp.sum(gradient * gradient)
    obs_cost, back_cost = lax.psum((obs_part, back_part), ("tm", "space"))
    grad_sq = lax.psum(grad_part, ("tm", "space"))
    total_cost = back_cost + obs_cost
    step_size = 0.5 * total_cost / (grad_sq + 1e-06)
    control = control - step_size * gradient
    cost_list = [total_cost]
    return (control, jnp.stack(cost_list))


LANES = 128
FOLD = 4
MESH_ID = pl.DeviceIdType.MESH
F32 = jnp.float32
BF16 = jnp.bfloat16


def basis64(n):
    k = np.arange(n, dtype=np.float64)[:, None]
    x = np.arange(n, dtype=np.float64)[None, :]
    c = np.sqrt(2.0 / n) * np.cos(np.pi * (x + 0.5) * k / n)
    c[0] *= np.sqrt(0.5)
    return c.astype(np.float32)


def folded_bases():
    cx, cy = basis64(GX), basis64(GY)
    order = np.arange(GX).reshape(GX // FOLD, FOLD).T.reshape(-1)
    cxp = cx[order][:, order]
    return [np.ascontiguousarray(a).astype(ml_dtypes.bfloat16) for a in (cxp, cxp.T, cy, cy.T)]


def mm(a, b):
    return jnp.dot(a, b, preferred_element_type=F32)


def unfold(wide):
    return jnp.concatenate([wide[:, r * GY : (r + 1) * GY] for r in range(FOLD)], axis=0)


def fold(tall):
    q = GX // FOLD
    return jnp.concatenate([tall[r * q : (r + 1) * q] for r in range(FOLD)], axis=1)


def xor_of(bits, k):
    return sum(lax.rem(b + lax.rem(lax.div(k, 1 << i), 2), 2) * (1 << i) for i, b in enumerate(bits))


def gather_lanes(rows, lanes):
    return jnp.take_along_axis(rows, lanes, axis=1, mode="promise_in_bounds")


def step_kernel(nt, ns, n_in, *refs):
    sources, (out, cost_out), held = refs[:n_in], refs[n_in : n_in + 2], refs[n_in + 2 :]
    landed, in_sem, held = held[:n_in], held[n_in], held[n_in + 1 :]
    control, spectrum, cy, cxpt, index, perturb, innov, sigma, qc, cxp, cyt = landed
    (
    flat, send_f, recv_f, spread, table, hi_hot, lo_hot, upd, prod,
    send_a, recv_a, part, parts, sf_sem, rf_sem, sa_sem, ra_sem, sp_sem, rp_sem,
    ) = held
    n = nt * ns
    my_t, my_s = lax.axis_index("tm"), lax.axis_index("space")
    me = my_t * ns + my_s
    slots, levels, piece = sources[5].shape[0], sources[5].shape[2], sources[5].shape[3]
    rows = piece // LANES
    cells = rows * levels
    sent = rows + rows % 2
    pad_rows = send_f.shape[1]
    q, width = GX // FOLD, FOLD * GY
    tiles = width // LANES
    chunks = index.shape[0] // slots
    group = 8
    bits = [lax.rem(lax.div(me, 1 << i), 2) for i in range(n.bit_length() - 1)]
    n_groups = n // group
    cuts = (20, 10, 0) if rows > 20 else (0,)
    ends = (rows,) + cuts[:-1]
    ranges = [(a, b - a, b - a + (b - a) % 2) for a, b in zip(cuts, ends)]

    def device(peer):
        return (lax.div(peer, ns), lax.rem(peer, ns))

    def peer_of(k):
        return me + sum((1 - 2 * b) * (1 << i) for i, b in enumerate(bits) if k >> i & 1)

    def load(i):
        return pltpu.make_async_copy(sources[i], landed[i], in_sem.at[i])

    barrier = pltpu.get_barrier_semaphore()

    for k in range(n - 1, 0, -1):
        pl.semaphore_signal(
            barrier, inc=1, device_id=device(peer_of(k)), device_id_type=MESH_ID
        )
    for i in (0, 1, 2, 3, 4):
        load(i).start()

    def wide_of(ref):
        return jnp.concatenate(
            [ref[pl.ds(a, q, stride=tiles), :] for a in range(tiles)], axis=1
        )

    def flat_from(wide):
        for a in range(tiles):
            flat[pl.ds(a, q, stride=tiles), :] = wide[:, a * LANES : (a + 1) * LANES]

    for i in (0, 1, 2):
        load(i).wait()
    ctl = wide_of(control)
    spec = wide_of(spectrum)
    mid = mm(unfold((ctl * spec).astype(BF16)), cy[...]).astype(BF16)
    load(3).wait()
    flat_from(fold(mm(cxpt[...], mid)))
    flat[q * tiles :, :] = jnp.zeros((flat.shape[0] - q * tiles, LANES), F32)
    for s in range(ns):
        send_f[s] = flat[s * rows : s * rows + pad_rows, :].astype(BF16)

    pl.semaphore_wait(barrier, n - 1)

    def f_copy(p, k):
        peer = peer_of(k)
        t, s = device(peer)
        at = pl.ds(ranges[p][0], ranges[p][2])
        return pltpu.make_async_remote_copy(
            send_f.at[s, at], recv_f.at[me, at], sf_sem, rf_sem.at[p * n_groups + k // group],
            device_id=(t, s), device_id_type=MESH_ID,
        )

    for p in range(len(ranges)):
        for k in range(n - 1, 0, -1):
            f_copy(p, k).start()
    recv_f[me] = send_f[my_s]

    for j in range(rows):
        pltpu.make_async_copy(
            sources[5].at[:, :, :, pl.ds(j * LANES, LANES)],
            perturb.at[:, :, pl.ds(j * levels, levels), :], in_sem.at[5],
        ).start()
    for i in range(6, n_in):
        load(i).start()

    back = 0.5 * jnp.sum(ctl * ctl, axis=0, keepdims=True)
    back = sum(back[:, a * LANES : (a + 1) * LANES] for a in range(tiles))
    table[...] = jnp.zeros(table.shape, F32)
    send_a[...] = jnp.zeros(send_a.shape, BF16)
    load(4).wait()
    hi_rows, lo_cols = hi_hot.shape[1], lo_hot.shape[2]
    his, los = [], []
    for t in range(slots):
        ix = index[pl.ds(t, chunks, stride=slots), :]
        level, point = ix // piece, ix % piece
        hi, lo = (point // LANES) * levels + level, point % LANES
        his.append(hi)
        los.append(lo)
        col = lo.T
        for c in range(chunks):
            at = pl.ds(c * LANES, LANES)
            hi_hot[t, :, at] = jnp.where(
                lax.broadcasted_iota(jnp.int32, (hi_rows, LANES), 0) == hi[c : c + 1, :], 1.0, 0.0
            ).astype(BF16)
            lo_hot[t, at, :] = jnp.where(
                lax.broadcasted_iota(jnp.int32, (LANES, lo_cols), 1) == col[:, c : c + 1], 1.0, 0.0
            ).astype(BF16)
    whole = perturb.at[:, :, pl.ds(0, cells), :]
    pltpu.make_async_copy(whole, whole, in_sem.at[5]).wait()

    block_bits = bits[group.bit_length() - 1 :]

    for i in (6, 7, 8):
        load(i).wait()
    models = [jnp.zeros((chunks, LANES), F32) for t in range(slots)]
    known = []
    for t in range(slots):
        mine = pl.ds(t, chunks, stride=slots)
        qct = qc[mine, :]
        rad = jnp.where(qct == 0, 4.0, jnp.where(qct == 1, 2.0, 1.0)).astype(F32)
        known.append((rad, 1.0 / (rad * rad), innov[mine, :], 1.0 / sigma[mine, :]))

    def add_group(p, g, own):
        r0, real, wide = ranges[p]
        at = pl.ds(r0 * levels, real * levels)
        block = xor_of(block_bits, g)
        arrived = recv_f.at[pl.ds(0, group - own), pl.ds(0, wide)]
        pltpu.make_async_copy(arrived, arrived, rf_sem.at[p * n_groups + g]).wait()
        for i in range(group):
            f = recv_f[block * group + i, r0:, :].astype(F32)[:real]
            for l in range(levels):
                spread[i, pl.ds(r0 * levels + l, real, stride=levels), :] = f
        for t in range(slots):
            total = table[t, at, :]
            for i in range(group):
                v = perturb[t, block * group + i, at, :].astype(F32)
                total = total + v * spread[i, at, :]
            table[t, at, :] = total

    def increments(p):
        add_group(p, 0, 1)

        def next_group(i, c):
            g = lax.rem(2 * i, n_groups) + lax.div(2 * i, n_groups)
            add_group(p, g, 0)
            return c

        lax.fori_loop(1, n_groups, next_group, 0)

    costs = [None] * slots

    def observe(p):
        r0, real, wide = ranges[p]
        top = hi_rows if r0 + real == rows else (r0 + real) * levels
        for t in range(slots):
            for h in range(r0 * levels, (r0 + real) * levels):
                picked = gather_lanes(
                    jnp.broadcast_to(table[t, h : h + 1, :], (chunks, LANES)), los[t]
                )
                models[t] = jnp.where(his[t] == h, picked, models[t])
            rad, bent, seen, inv = known[t]
            scaled = (models[t] - seen) * inv
            sq = scaled * scaled * bent
            costs[t] = (rad, sq)
            g = scaled * inv / (1.0 + sq)
            terms = jnp.concatenate(
                [
                    hi_hot[t, r0 * levels : top, c * LANES : (c + 1) * LANES]
                    * jnp.broadcast_to(g[c : c + 1, :], (top - r0 * levels, LANES)).astype(BF16)
                    for c in range(chunks)
                ],
                axis=1,
            )
            upd[t, r0 * levels : top, :] = mm(terms, lo_hot[t]).astype(BF16).astype(F32)

    def a_copy(p, peer, far):
        at = pl.ds(ranges[p][0], ranges[p][2])
        return pltpu.make_async_remote_copy(
            send_a.at[peer, at], recv_a.at[me, at], sa_sem, ra_sem.at[far],
            device_id=device(peer), device_id_type=MESH_ID,
        )

    def one_member(p, m, i, to):
        r0, real, wide = ranges[p]
        at = pl.ds(r0 * levels, real * levels)
        prod[i, at, :] = sum(
            perturb[t, m, at, :].astype(F32) * upd[t, at, :] for t in range(slots)
        )
        to[pl.ds(r0, real), :] = sum(
            prod[i, pl.ds(r0 * levels + l, real, stride=levels), :] for l in range(levels)
        ).astype(BF16)

    def low_of(i):
        return sum((1 - 2 * b) * (1 << j) for j, b in enumerate(bits[:3]) if i >> j & 1)

    def adjoints(p):
        def eight(d, c):
            base = xor_of(block_bits, n_groups - 1 - d) * group + lax.rem(me, group)
            peers = [base + low_of(i) for i in range(group - 1, -1, -1)]
            for i, peer in enumerate(peers):
                one_member(p, peer, i, send_a.at[peer])
            for peer in peers:
                a_copy(p, peer, lax.rem(n_groups - 1 - d, 2)).start()
            return c

        lax.fori_loop(0, n_groups - 1, eight, 0)
        peers = [peer_of(i) for i in range(group - 1, 0, -1)]
        for i, peer in enumerate(peers):
            one_member(p, peer, i, send_a.at[peer])
        one_member(p, me, group - 1, recv_a.at[me])
        for peer in peers:
            a_copy(p, peer, 0).start()

    for p in range(len(ranges)):
        increments(p)
        observe(p)
        adjoints(p)

    cost_row = back
    for rad, sq in costs:
        cost_row = cost_row + jnp.sum(0.5 * rad * rad * jnp.log1p(sq), axis=0, keepdims=True)
    part[0:1, :] = cost_row
    for i in (9, 10):
        load(i).wait()

    for far in (0, 1):
        pieces = n // 2 - 1 + far
        arrived = recv_a.at[pl.ds(0, pieces), pl.ds(0, sent)]
        pltpu.make_async_copy(arrived, arrived, ra_sem.at[far]).wait()
        half = lax.rem(block_bits[0] + far, 2)
        for i in range(ns // 2):
            s = half * (ns // 2) + i
            at = pl.multiple_of(half * (ns // 2 * rows), 8) + i * rows
            flat[pl.ds(at, rows), :] = sum(
                recv_a[t * ns + s].astype(F32)[:rows] for t in range(nt)
            )
    mid = mm(cxp[...], unfold(wide_of(flat).astype(BF16))).astype(BF16)
    gr = ctl + spec * fold(mm(mid, cyt[...]))
    sq = jnp.sum(gr * gr, axis=0, keepdims=True)
    part[1:2, :] = sum(sq[:, a * LANES : (a + 1) * LANES] for a in range(tiles))

    def s_copy(k):
        peer = peer_of(k)
        return pltpu.make_async_remote_copy(
            part, parts.at[me], sp_sem, rp_sem, device_id=device(peer), device_id_type=MESH_ID,
        )

    for k in range(n - 1, 0, -1):
        s_copy(k).start()
    parts[me] = part[...]
    flat_from(gr)
    all_sent = send_a.at[pl.ds(0, n - 1), pl.ds(0, sent)]
    pltpu.make_async_copy(all_sent, all_sent, sf_sem).wait()
    pltpu.make_async_copy(all_sent, all_sent, sa_sem).wait()

    all_parts = parts.at[pl.ds(0, n - 1)]
    pltpu.make_async_copy(all_parts, all_parts, sp_sem).wait()
    pltpu.make_async_copy(all_parts, all_parts, rp_sem).wait()
    sums = jnp.sum(jnp.sum(parts[...], axis=0), axis=1, keepdims=True)
    total_cost, grad_sq = sums[0:1, :], sums[1:2, :]
    step = 0.5 * total_cost / (grad_sq + 1e-06)
    out[...] = control[...] - step * flat[: q * tiles, :]
    cost_out[...] = jnp.broadcast_to(total_cost, cost_out.shape)


def put_kernel(out, cost, out_to, cost_to, sem):
    copies = [
        pltpu.make_async_copy(src, dst, sem.at[i])
        for i, (src, dst) in enumerate(((out, out_to), (cost, cost_to)))
    ]
    for copy in copies:
        copy.start()
    for copy in copies:
        copy.wait()


def fused_device(nt, ns, control, spectrum, perturb, obs_index, innovation, obs_sigma, qc_class):
    n = nt * ns
    slots, members, levels, piece = perturb.shape
    grid_rows = GX * GY // LANES
    rows = piece // LANES
    cells = rows * levels
    pad_rows = -(-rows // 16) * 16
    pad_cells = -(-cells // 16) * 16
    hi_rows = pad_cells
    obs = obs_index.shape[1]
    vm = pl.BlockSpec(memory_space=pltpu.VMEM)
    dma = pltpu.SemaphoreType.DMA
    cxp, cxpt, cy, cyt = [jnp.asarray(b) for b in folded_bases()]

    def by_chunk(x):
        return x.reshape(slots, obs // LANES, LANES).transpose(1, 0, 2).reshape(-1, LANES)

    sources = [
        control.reshape(grid_rows, LANES), spectrum.reshape(grid_rows, LANES), cy, cxpt,
        by_chunk(obs_index), perturb, by_chunk(innovation), by_chunk(obs_sigma),
        by_chunk(qc_class), cxp, cyt,
    ]
    lands = [pltpu.VMEM(a.shape, a.dtype) for a in sources]
    lands[5] = pltpu.VMEM((slots, members, pad_cells, LANES), BF16)
    out, cost = pl.pallas_call(
        functools.partial(step_kernel, nt, ns, len(sources)),
        out_shape=(
            jax.ShapeDtypeStruct((grid_rows, LANES), F32),
            jax.ShapeDtypeStruct((1, LANES), F32),
        ),
        in_specs=[pl.BlockSpec(memory_space=pltpu.HBM)] * len(sources),
        out_specs=(vm, vm),
        scratch_shapes=[
            *lands,
            dma((len(sources),)),
            pltpu.VMEM((grid_rows + 16, LANES), F32),
            pltpu.VMEM((ns, pad_rows, LANES), BF16),
            pltpu.VMEM((n, pad_rows, LANES), BF16),
            pltpu.VMEM((8, pad_cells, LANES), F32),
            pltpu.VMEM((slots, pad_cells, LANES), F32),
            pltpu.VMEM((slots, hi_rows, obs), BF16),
            pltpu.VMEM((slots, obs, LANES), BF16),
            pltpu.VMEM((slots, pad_cells, LANES), F32),
            pltpu.VMEM((8, pad_cells, LANES), F32),
            pltpu.VMEM((n, pad_rows, LANES), BF16),
            pltpu.VMEM((n, pad_rows, LANES), BF16),
            pltpu.VMEM((2, LANES), F32),
            pltpu.VMEM((n, 2, LANES), F32),
            dma, dma((3 * n // 8,)), dma, dma((2,)), dma, dma,
        ],
        compiler_params=pltpu.CompilerParams(
            collective_id=0, has_side_effects=True, vmem_limit_bytes=24 << 20
        ),
        name="envar_step",
    )(*[pltpu.with_memory_space_constraint(a, pltpu.HBM) for a in sources])
    out, cost = pl.pallas_call(
        put_kernel,
        out_shape=(
            jax.ShapeDtypeStruct((grid_rows, LANES), F32),
            jax.ShapeDtypeStruct((1, LANES), F32),
        ),
        in_specs=[pl.BlockSpec(memory_space=pltpu.VMEM)] * 2,
        out_specs=[pl.BlockSpec(memory_space=pltpu.HBM)] * 2,
        scratch_shapes=[dma((2,))],
        name="put_results",
    )(*[pltpu.with_memory_space_constraint(a, pltpu.VMEM) for a in (out, cost)])
    return out.reshape(control.shape), cost[0, :1]


def fused_fits(nt, ns, control, perturb, innovation):
    n = nt * ns
    piece = GX * GY // ns
    return (
        nt == 2
        and ns == 16
        and control.shape[0] == n
        and perturb.shape[2] == 4
        and piece % LANES == 0
        and (FOLD * GY) % LANES == 0
        and (GX // FOLD) % 8 == 0
        and innovation.shape[1] // ns == 16 * LANES
    )


def solution(mesh):
    nt, ns = mesh.shape["tm"], mesh.shape["space"]

    def whole(control, spectrum, perturb, obs_index, innovation, obs_sigma, qc_class):
        fits = fused_fits(nt, ns, control, perturb, innovation)
        body = functools.partial(fused_device, nt, ns) if fits else per_device
        return on_mesh(mesh, body)(
            control, spectrum, perturb, obs_index, innovation, obs_sigma, qc_class
        )

    return whole


def on_mesh(mesh, body):
    in_specs = (
        P(("tm", "space"), None),
        P(),
        P("tm", None, None, "space"),
        P("tm", "space"),
        P("tm", "space"),
        P("tm", "space"),
        P("tm", "space"),
    )
    out_specs = (P(("tm", "space"), None), P())
    return jax.shard_map(
        body, mesh=mesh, in_specs=in_specs, out_specs=out_specs, check_vma=False
    )
```

```python
import functools

import jax
import jax.numpy as jnp
import ml_dtypes
import numpy as np
from jax import lax
from jax.experimental import pallas as pl
from jax.experimental.pallas import tpu as pltpu
from jax.sharding import PartitionSpec as P

GX = 320
GY = 160


def lookup_tables(segment_length):
    wave_num = jnp.arange(segment_length, dtype=jnp.float32)[:, None]
    grid_positions = jnp.arange(segment_length, dtype=jnp.float32)[None, :]
    basis = jnp.cos(jnp.pi * (grid_positions + 0.5) * wave_num / segment_length) * jnp.sqrt(
        2.0 / segment_length
    )
    return jnp.where(wave_num == 0, basis * jnp.sqrt(0.5), basis)


def synthesize(control, spectrum, basis_x, basis_y):
    coeffs = (control * spectrum[None, :]).reshape(control.shape[0], GX, GY)
    middle = jnp.einsum("kn,mkl->mnl", basis_x, coeffs, precision=lax.Precision.HIGHEST)
    result = jnp.einsum("mnl,lp->mnp", middle, basis_y, precision=lax.Precision.HIGHEST)
    return result.reshape(control.shape[0], GX * GY)


def analyze(adjoint, spectrum, basis_x, basis_y):
    state_fields = adjoint.reshape(adjoint.shape[0], GX, GY)
    middle = jnp.einsum("kn,mnp->mkp", basis_x, state_fields, precision=lax.Precision.HIGHEST)
    result = jnp.einsum("mkp,lp->mkl", middle, basis_y, precision=lax.Precision.HIGHEST)
    return result.reshape(adjoint.shape[0], GX * GY) * spectrum[None, :]


def per_device(control, spectrum, perturb, obs_index, innovation, obs_sigma, qc_class):
    basis_x = lookup_tables(GX)
    basis_y = lookup_tables(GY)
    slot_count = perturb.shape[0]
    levels = perturb.shape[2]
    piece_len = perturb.shape[3]
    radius = jnp.where(qc_class == 0, 4.0, jnp.where(qc_class == 1, 2.0, 1.0)).astype(jnp.float32)

    def scatter_cells(indices, values):
        return jnp.zeros((levels * piece_len,), jnp.float32).at[indices].add(values)

    member_field = synthesize(control, spectrum, basis_x, basis_y).astype(jnp.bfloat16)
    pieces = lax.all_to_all(member_field, "space", split_axis=1, concat_axis=0, tiled=True)
    selected_entries = perturb
    increment = jnp.einsum(
        "dzab,zb->dab",
        selected_entries,
        lax.all_gather(pieces, "tm", axis=0, tiled=True),
        preferred_element_type=jnp.float32,
    )
    cells_flat = increment.reshape(slot_count, levels * piece_len)
    modelled = jnp.take_along_axis(cells_flat, obs_index, axis=1)
    scaled = (modelled - innovation) / obs_sigma
    scaled_sq = scaled * scaled / (radius * radius)
    obs_part = jnp.sum(0.5 * radius * radius * jnp.log1p(scaled_sq))
    back_part = 0.5 * jnp.sum(control * control)
    obs_grad = scaled / ((1.0 + scaled_sq) * obs_sigma)
    control_update = jax.vmap(scatter_cells)(obs_index, obs_grad).astype(jnp.bfloat16)
    control_update = control_update.reshape(slot_count, levels, piece_len)
    selected_entries = perturb
    summed_rows = lax.psum_scatter(
        jnp.einsum(
            "qiyr,qyr->ir", selected_entries, control_update, preferred_element_type=jnp.float32
        ).astype(jnp.bfloat16),
        "tm",
        scatter_dimension=0,
        tiled=True,
    ).astype(jnp.float32)
    adjoint = lax.all_to_all(
        summed_rows.astype(jnp.bfloat16), "space", split_axis=0, concat_axis=1, tiled=True
    ).astype(summed_rows.dtype)
    gradient = control + analyze(adjoint, spectrum, basis_x, basis_y)
    grad_part = jnp.sum(gradient * gradient)
    obs_cost, back_cost = lax.psum((obs_part, back_part), ("tm", "space"))
    grad_sq = lax.psum(grad_part, ("tm", "space"))
    total_cost = back_cost + obs_cost
    step_size = 0.5 * total_cost / (grad_sq + 1e-06)
    control = control - step_size * gradient
    cost_list = [total_cost]
    return (control, jnp.stack(cost_list))


LANES = 128
FOLD = 4
MESH_ID = pl.DeviceIdType.MESH
F32 = jnp.float32
BF16 = jnp.bfloat16


def basis64(n):
    k = np.arange(n, dtype=np.float64)[:, None]
    x = np.arange(n, dtype=np.float64)[None, :]
    c = np.sqrt(2.0 / n) * np.cos(np.pi * (x + 0.5) * k / n)
    c[0] *= np.sqrt(0.5)
    return c.astype(np.float32)


def folded_bases():
    cx, cy = basis64(GX), basis64(GY)
    order = np.arange(GX).reshape(GX // FOLD, FOLD).T.reshape(-1)
    cxp = cx[order][:, order]
    return [np.ascontiguousarray(a).astype(ml_dtypes.bfloat16) for a in (cxp, cxp.T, cy, cy.T)]


def mm(a, b):
    return jnp.dot(a, b, preferred_element_type=F32)


def unfold(wide):
    return jnp.concatenate([wide[:, r * GY : (r + 1) * GY] for r in range(FOLD)], axis=0)


def fold(tall):
    q = GX // FOLD
    return jnp.concatenate([tall[r * q : (r + 1) * q] for r in range(FOLD)], axis=1)


def xor_of(bits, k):
    return sum(lax.rem(b + lax.rem(lax.div(k, 1 << i), 2), 2) * (1 << i) for i, b in enumerate(bits))


def gather_lanes(rows, lanes):
    return jnp.take_along_axis(rows, lanes, axis=1, mode="promise_in_bounds")


def step_kernel(nt, ns, n_in, *refs):
    sources, (out, cost_out), held = refs[:n_in], refs[n_in : n_in + 2], refs[n_in + 2 :]
    landed, in_sem, held = held[:n_in], held[n_in], held[n_in + 1 :]
    control, spectrum, cy, cxpt, index, perturb, innov, sigma, qc, cxp, cyt = landed
    (
    flat, send_f, recv_f, spread, table, hi_hot, lo_hot, upd, prod,
    send_a, recv_a, part, parts, sf_sem, rf_sem, sa_sem, ra_sem, sp_sem, rp_sem,
    ) = held
    n = nt * ns
    my_t, my_s = lax.axis_index("tm"), lax.axis_index("space")
    me = my_t * ns + my_s
    slots, levels, piece = sources[5].shape[0], sources[5].shape[2], sources[5].shape[3]
    rows = piece // LANES
    cells = rows * levels
    sent = rows + rows % 2
    pad_rows = send_f.shape[1]
    q, width = GX // FOLD, FOLD * GY
    tiles = width // LANES
    chunks = index.shape[0] // slots
    group = 8
    bits = [lax.rem(lax.div(me, 1 << i), 2) for i in range(n.bit_length() - 1)]
    n_groups = n // group
    cuts = (20, 12, 0) if rows > 20 else (0,)
    ends = (rows,) + cuts[:-1]
    ranges = [(a, b - a, b - a + (b - a) % 2) for a, b in zip(cuts, ends)]

    def device(peer):
        return (lax.div(peer, ns), lax.rem(peer, ns))

    def peer_of(k):
        return me + sum((1 - 2 * b) * (1 << i) for i, b in enumerate(bits) if k >> i & 1)

    def load(i):
        return pltpu.make_async_copy(sources[i], landed[i], in_sem.at[i])

    for i in (0, 1, 2, 3):
        load(i).start()

    barrier = pltpu.get_barrier_semaphore()

    for k in range(n - 1, 0, -1):
        pl.semaphore_signal(
            barrier, inc=1, device_id=device(peer_of(k)), device_id_type=MESH_ID
        )
    load(4).start()

    def wide_of(ref):
        return jnp.concatenate(
            [ref[pl.ds(a, q, stride=tiles), :] for a in range(tiles)], axis=1
        )

    def flat_from(wide):
        for a in range(tiles):
            flat[pl.ds(a, q, stride=tiles), :] = wide[:, a * LANES : (a + 1) * LANES]

    for i in (0, 1, 2):
        load(i).wait()
    ctl = wide_of(control)
    spec = wide_of(spectrum)
    mid = mm(unfold((ctl * spec).astype(BF16)), cy[...]).astype(BF16)
    load(3).wait()
    flat_from(fold(mm(cxpt[...], mid)))
    flat[q * tiles :, :] = jnp.zeros((flat.shape[0] - q * tiles, LANES), F32)
    for s in range(ns):
        send_f[s] = flat[s * rows : s * rows + pad_rows, :].astype(BF16)

    pl.semaphore_wait(barrier, n - 1)

    def f_copy(p, k):
        peer = peer_of(k)
        t, s = device(peer)
        at = pl.ds(ranges[p][0], ranges[p][2])
        return pltpu.make_async_remote_copy(
            send_f.at[s, at], recv_f.at[me, at], sf_sem, rf_sem.at[p * n_groups + k // group],
            device_id=(t, s), device_id_type=MESH_ID,
        )

    for p in range(len(ranges)):
        for k in range(n - 1, 0, -1):
            f_copy(p, k).start()
    recv_f[me] = send_f[my_s]

    for j in range(rows):
        pltpu.make_async_copy(
            sources[5].at[:, :, :, pl.ds(j * LANES, LANES)],
            perturb.at[:, :, pl.ds(j * levels, levels), :], in_sem.at[5],
        ).start()
    for i in range(6, n_in):
        load(i).start()

    back = 0.5 * jnp.sum(ctl * ctl, axis=0, keepdims=True)
    back = sum(back[:, a * LANES : (a + 1) * LANES] for a in range(tiles))
    table[...] = jnp.zeros(table.shape, F32)
    send_a[...] = jnp.zeros(send_a.shape, BF16)
    load(4).wait()
    hi_rows, lo_cols = hi_hot.shape[1], lo_hot.shape[2]
    his, los = [], []
    for t in range(slots):
        ix = index[pl.ds(t, chunks, stride=slots), :]
        level, point = ix // piece, ix % piece
        hi, lo = (point // LANES) * levels + level, point % LANES
        his.append(hi)
        los.append(lo)
        col = lo.T
        for c in range(chunks):
            at = pl.ds(c * LANES, LANES)
            hi_hot[t, :, at] = jnp.where(
                lax.broadcasted_iota(jnp.int32, (hi_rows, LANES), 0) == hi[c : c + 1, :], 1.0, 0.0
            ).astype(BF16)
            lo_hot[t, at, :] = jnp.where(
                lax.broadcasted_iota(jnp.int32, (LANES, lo_cols), 1) == col[:, c : c + 1], 1.0, 0.0
            ).astype(BF16)
    whole = perturb.at[:, :, pl.ds(0, cells), :]
    pltpu.make_async_copy(whole, whole, in_sem.at[5]).wait()

    block_bits = bits[group.bit_length() - 1 :]

    for i in (6, 7, 8):
        load(i).wait()
    models = [jnp.zeros((chunks, LANES), F32) for t in range(slots)]
    known = []
    for t in range(slots):
        mine = pl.ds(t, chunks, stride=slots)
        qct = qc[mine, :]
        rad = jnp.where(qct == 0, 4.0, jnp.where(qct == 1, 2.0, 1.0)).astype(F32)
        known.append((rad, 1.0 / (rad * rad), innov[mine, :], 1.0 / sigma[mine, :]))

    def add_group(p, g, own):
        r0, real, wide = ranges[p]
        at = pl.ds(r0 * levels, real * levels)
        block = xor_of(block_bits, g)
        arrived = recv_f.at[pl.ds(0, group - own), pl.ds(0, wide)]
        pltpu.make_async_copy(arrived, arrived, rf_sem.at[p * n_groups + g]).wait()
        for i in range(group):
            f = recv_f[block * group + i, r0:, :].astype(F32)[:real]
            for l in range(levels):
                spread[i, pl.ds(r0 * levels + l, real, stride=levels), :] = f
        for t in range(slots):
            total = table[t, at, :]
            for i in range(group):
                v = perturb[t, block * group + i, at, :].astype(F32)
                total = total + v * spread[i, at, :]
            table[t, at, :] = total

    def increments(p):
        add_group(p, 0, 1)

        def next_group(i, c):
            g = lax.rem(2 * i, n_groups) + lax.div(2 * i, n_groups)
            add_group(p, g, 0)
            return c

        lax.fori_loop(1, n_groups, next_group, 0)

    costs = [None] * slots

    def observe(p):
        r0, real, wide = ranges[p]
        top = hi_rows if r0 + real == rows else (r0 + real) * levels
        for t in range(slots):
            for h in range(r0 * levels, (r0 + real) * levels):
                picked = gather_lanes(
                    jnp.broadcast_to(table[t, h : h + 1, :], (chunks, LANES)), los[t]
                )
                models[t] = jnp.where(his[t] == h, picked, models[t])
            rad, bent, seen, inv = known[t]
            scaled = (models[t] - seen) * inv
            sq = scaled * scaled * bent
            costs[t] = (rad, sq)
            g = scaled * inv / (1.0 + sq)
            terms = jnp.concatenate(
                [
                    hi_hot[t, r0 * levels : top, c * LANES : (c + 1) * LANES]
                    * jnp.broadcast_to(g[c : c + 1, :], (top - r0 * levels, LANES)).astype(BF16)
                    for c in range(chunks)
                ],
                axis=1,
            )
            upd[t, r0 * levels : top, :] = mm(terms, lo_hot[t]).astype(BF16).astype(F32)

    def a_copy(p, peer, far):
        at = pl.ds(ranges[p][0], ranges[p][2])
        return pltpu.make_async_remote_copy(
            send_a.at[peer, at], recv_a.at[me, at], sa_sem, ra_sem.at[far],
            device_id=device(peer), device_id_type=MESH_ID,
        )

    def one_member(p, m, i, to):
        r0, real, wide = ranges[p]
        at = pl.ds(r0 * levels, real * levels)
        prod[i, at, :] = sum(
            perturb[t, m, at, :].astype(F32) * upd[t, at, :] for t in range(slots)
        )
        to[pl.ds(r0, real), :] = sum(
            prod[i, pl.ds(r0 * levels + l, real, stride=levels), :] for l in range(levels)
        ).astype(BF16)

    def low_of(i):
        return sum((1 - 2 * b) * (1 << j) for j, b in enumerate(bits[:3]) if i >> j & 1)

    def adjoints(p):
        def eight(d, c):
            base = xor_of(block_bits, n_groups - 1 - d) * group + lax.rem(me, group)
            peers = [base + low_of(i) for i in range(group - 1, -1, -1)]
            for i, peer in enumerate(peers):
                one_member(p, peer, i, send_a.at[peer])
            for peer in peers:
                a_copy(p, peer, lax.rem(n_groups - 1 - d, 2)).start()
            return c

        lax.fori_loop(0, n_groups - 1, eight, 0)
        peers = [peer_of(i) for i in range(group - 1, 0, -1)]
        for i, peer in enumerate(peers):
            one_member(p, peer, i, send_a.at[peer])
        one_member(p, me, group - 1, recv_a.at[me])
        for peer in peers:
            a_copy(p, peer, 0).start()

    for p in range(len(ranges)):
        increments(p)
        observe(p)
        adjoints(p)

    cost_row = back
    for rad, sq in costs:
        cost_row = cost_row + jnp.sum(0.5 * rad * rad * jnp.log1p(sq), axis=0, keepdims=True)
    part[0:1, :] = cost_row
    for i in (9, 10):
        load(i).wait()

    for far in (0, 1):
        pieces = n // 2 - 1 + far
        arrived = recv_a.at[pl.ds(0, pieces), pl.ds(0, sent)]
        pltpu.make_async_copy(arrived, arrived, ra_sem.at[far]).wait()
        half = lax.rem(block_bits[0] + far, 2)
        for i in range(ns // 2):
            s = half * (ns // 2) + i
            at = pl.multiple_of(half * (ns // 2 * rows), 8) + i * rows
            flat[pl.ds(at, rows), :] = sum(
                recv_a[t * ns + s].astype(F32)[:rows] for t in range(nt)
            )
    mid = mm(cxp[...], unfold(wide_of(flat).astype(BF16))).astype(BF16)
    gr = ctl + spec * fold(mm(mid, cyt[...]))
    sq = jnp.sum(gr * gr, axis=0, keepdims=True)
    part[1:2, :] = sum(sq[:, a * LANES : (a + 1) * LANES] for a in range(tiles))

    def s_copy(k):
        peer = peer_of(k)
        return pltpu.make_async_remote_copy(
            part, parts.at[me], sp_sem, rp_sem, device_id=device(peer), device_id_type=MESH_ID,
        )

    for k in range(n - 1, 0, -1):
        s_copy(k).start()
    parts[me] = part[...]
    flat_from(gr)
    all_sent = send_a.at[pl.ds(0, n - 1), pl.ds(0, sent)]
    pltpu.make_async_copy(all_sent, all_sent, sf_sem).wait()
    pltpu.make_async_copy(all_sent, all_sent, sa_sem).wait()

    all_parts = parts.at[pl.ds(0, n - 1)]
    pltpu.make_async_copy(all_parts, all_parts, sp_sem).wait()
    pltpu.make_async_copy(all_parts, all_parts, rp_sem).wait()
    sums = [parts[i] for i in range(n)]
    while len(sums) > 1:
        sums = [a + b for a, b in zip(sums[::2], sums[1::2])]
    sums = jnp.sum(sums[0], axis=1, keepdims=True)
    total_cost, grad_sq = sums[0:1, :], sums[1:2, :]
    step = 0.5 * total_cost / (grad_sq + 1e-06)
    out[...] = control[...] - step * flat[: q * tiles, :]
    cost_out[...] = jnp.broadcast_to(total_cost, cost_out.shape)


def put_kernel(out, cost, out_to, cost_to, sem):
    copies = [
        pltpu.make_async_copy(src, dst, sem.at[i])
        for i, (src, dst) in enumerate(((out, out_to), (cost, cost_to)))
    ]
    for copy in copies:
        copy.start()
    for copy in copies:
        copy.wait()


def fused_device(nt, ns, control, spectrum, perturb, obs_index, innovation, obs_sigma, qc_class):
    n = nt * ns
    slots, members, levels, piece = perturb.shape
    grid_rows = GX * GY // LANES
    rows = piece // LANES
    cells = rows * levels
    pad_rows = -(-rows // 16) * 16
    pad_cells = -(-cells // 16) * 16
    hi_rows = pad_cells
    obs = obs_index.shape[1]
    vm = pl.BlockSpec(memory_space=pltpu.VMEM)
    dma = pltpu.SemaphoreType.DMA
    cxp, cxpt, cy, cyt = [jnp.asarray(b) for b in folded_bases()]

    def by_chunk(x):
        return x.reshape(slots, obs // LANES, LANES).transpose(1, 0, 2).reshape(-1, LANES)

    sources = [
        control.reshape(grid_rows, LANES), spectrum.reshape(grid_rows, LANES), cy, cxpt,
        by_chunk(obs_index), perturb, by_chunk(innovation), by_chunk(obs_sigma),
        by_chunk(qc_class), cxp, cyt,
    ]
    lands = [pltpu.VMEM(a.shape, a.dtype) for a in sources]
    lands[5] = pltpu.VMEM((slots, members, pad_cells, LANES), BF16)
    out, cost = pl.pallas_call(
        functools.partial(step_kernel, nt, ns, len(sources)),
        out_shape=(
            jax.ShapeDtypeStruct((grid_rows, LANES), F32),
            jax.ShapeDtypeStruct((1, LANES), F32),
        ),
        in_specs=[pl.BlockSpec(memory_space=pltpu.HBM)] * len(sources),
        out_specs=(vm, vm),
        scratch_shapes=[
            *lands,
            dma((len(sources),)),
            pltpu.VMEM((grid_rows + 16, LANES), F32),
            pltpu.VMEM((ns, pad_rows, LANES), BF16),
            pltpu.VMEM((n, pad_rows, LANES), BF16),
            pltpu.VMEM((8, pad_cells, LANES), F32),
            pltpu.VMEM((slots, pad_cells, LANES), F32),
            pltpu.VMEM((slots, hi_rows, obs), BF16),
            pltpu.VMEM((slots, obs, LANES), BF16),
            pltpu.VMEM((slots, pad_cells, LANES), F32),
            pltpu.VMEM((8, pad_cells, LANES), F32),
            pltpu.VMEM((n, pad_rows, LANES), BF16),
            pltpu.VMEM((n, pad_rows, LANES), BF16),
            pltpu.VMEM((2, LANES), F32),
            pltpu.VMEM((n, 2, LANES), F32),
            dma, dma((3 * n // 8,)), dma, dma((2,)), dma, dma,
        ],
        compiler_params=pltpu.CompilerParams(
            collective_id=0, has_side_effects=True, vmem_limit_bytes=24 << 20
        ),
        name="envar_step",
    )(*[pltpu.with_memory_space_constraint(a, pltpu.HBM) for a in sources])
    out, cost = pl.pallas_call(
        put_kernel,
        out_shape=(
            jax.ShapeDtypeStruct((grid_rows, LANES), F32),
            jax.ShapeDtypeStruct((1, LANES), F32),
        ),
        in_specs=[pl.BlockSpec(memory_space=pltpu.VMEM)] * 2,
        out_specs=[pl.BlockSpec(memory_space=pltpu.HBM)] * 2,
        scratch_shapes=[dma((2,))],
        name="put_results",
    )(*[pltpu.with_memory_space_constraint(a, pltpu.VMEM) for a in (out, cost)])
    return out.reshape(control.shape), cost[0, :1]


def fused_fits(nt, ns, control, perturb, innovation):
    n = nt * ns
    piece = GX * GY // ns
    return (
        nt == 2
        and ns == 16
        and control.shape[0] == n
        and perturb.shape[2] == 4
        and piece % LANES == 0
        and (FOLD * GY) % LANES == 0
        and (GX // FOLD) % 8 == 0
        and innovation.shape[1] // ns == 16 * LANES
    )


def solution(mesh):
    nt, ns = mesh.shape["tm"], mesh.shape["space"]

    def whole(control, spectrum, perturb, obs_index, innovation, obs_sigma, qc_class):
        fits = fused_fits(nt, ns, control, perturb, innovation)
        body = functools.partial(fused_device, nt, ns) if fits else per_device
        return on_mesh(mesh, body)(
            control, spectrum, perturb, obs_index, innovation, obs_sigma, qc_class
        )

    return whole


def on_mesh(mesh, body):
    in_specs = (
        P(("tm", "space"), None),
        P(),
        P("tm", None, None, "space"),
        P("tm", "space"),
        P("tm", "space"),
        P("tm", "space"),
        P("tm", "space"),
    )
    out_specs = (P(("tm", "space"), None), P())
    return jax.shard_map(
        body, mesh=mesh, in_specs=in_specs, out_specs=out_specs, check_vma=False
    )
```

```python
import functools

import jax
import jax.numpy as jnp
import ml_dtypes
import numpy as np
from jax import lax
from jax.experimental import pallas as pl
from jax.experimental.pallas import tpu as pltpu
from jax.sharding import PartitionSpec as P

GX = 320
GY = 160


def lookup_tables(segment_length):
    wave_num = jnp.arange(segment_length, dtype=jnp.float32)[:, None]
    grid_positions = jnp.arange(segment_length, dtype=jnp.float32)[None, :]
    basis = jnp.cos(jnp.pi * (grid_positions + 0.5) * wave_num / segment_length) * jnp.sqrt(
        2.0 / segment_length
    )
    return jnp.where(wave_num == 0, basis * jnp.sqrt(0.5), basis)


def synthesize(control, spectrum, basis_x, basis_y):
    coeffs = (control * spectrum[None, :]).reshape(control.shape[0], GX, GY)
    middle = jnp.einsum("kn,mkl->mnl", basis_x, coeffs, precision=lax.Precision.HIGHEST)
    result = jnp.einsum("mnl,lp->mnp", middle, basis_y, precision=lax.Precision.HIGHEST)
    return result.reshape(control.shape[0], GX * GY)


def analyze(adjoint, spectrum, basis_x, basis_y):
    state_fields = adjoint.reshape(adjoint.shape[0], GX, GY)
    middle = jnp.einsum("kn,mnp->mkp", basis_x, state_fields, precision=lax.Precision.HIGHEST)
    result = jnp.einsum("mkp,lp->mkl", middle, basis_y, precision=lax.Precision.HIGHEST)
    return result.reshape(adjoint.shape[0], GX * GY) * spectrum[None, :]


def per_device(control, spectrum, perturb, obs_index, innovation, obs_sigma, qc_class):
    basis_x = lookup_tables(GX)
    basis_y = lookup_tables(GY)
    slot_count = perturb.shape[0]
    levels = perturb.shape[2]
    piece_len = perturb.shape[3]
    radius = jnp.where(qc_class == 0, 4.0, jnp.where(qc_class == 1, 2.0, 1.0)).astype(jnp.float32)

    def scatter_cells(indices, values):
        return jnp.zeros((levels * piece_len,), jnp.float32).at[indices].add(values)

    member_field = synthesize(control, spectrum, basis_x, basis_y).astype(jnp.bfloat16)
    pieces = lax.all_to_all(member_field, "space", split_axis=1, concat_axis=0, tiled=True)
    selected_entries = perturb
    increment = jnp.einsum(
        "dzab,zb->dab",
        selected_entries,
        lax.all_gather(pieces, "tm", axis=0, tiled=True),
        preferred_element_type=jnp.float32,
    )
    cells_flat = increment.reshape(slot_count, levels * piece_len)
    modelled = jnp.take_along_axis(cells_flat, obs_index, axis=1)
    scaled = (modelled - innovation) / obs_sigma
    scaled_sq = scaled * scaled / (radius * radius)
    obs_part = jnp.sum(0.5 * radius * radius * jnp.log1p(scaled_sq))
    back_part = 0.5 * jnp.sum(control * control)
    obs_grad = scaled / ((1.0 + scaled_sq) * obs_sigma)
    control_update = jax.vmap(scatter_cells)(obs_index, obs_grad).astype(jnp.bfloat16)
    control_update = control_update.reshape(slot_count, levels, piece_len)
    selected_entries = perturb
    summed_rows = lax.psum_scatter(
        jnp.einsum(
            "qiyr,qyr->ir", selected_entries, control_update, preferred_element_type=jnp.float32
        ).astype(jnp.bfloat16),
        "tm",
        scatter_dimension=0,
        tiled=True,
    ).astype(jnp.float32)
    adjoint = lax.all_to_all(
        summed_rows.astype(jnp.bfloat16), "space", split_axis=0, concat_axis=1, tiled=True
    ).astype(summed_rows.dtype)
    gradient = control + analyze(adjoint, spectrum, basis_x, basis_y)
    grad_part = jnp.sum(gradient * gradient)
    obs_cost, back_cost = lax.psum((obs_part, back_part), ("tm", "space"))
    grad_sq = lax.psum(grad_part, ("tm", "space"))
    total_cost = back_cost + obs_cost
    step_size = 0.5 * total_cost / (grad_sq + 1e-06)
    control = control - step_size * gradient
    cost_list = [total_cost]
    return (control, jnp.stack(cost_list))


LANES = 128
FOLD = 4
MESH_ID = pl.DeviceIdType.MESH
F32 = jnp.float32
BF16 = jnp.bfloat16


def basis64(n):
    k = np.arange(n, dtype=np.float64)[:, None]
    x = np.arange(n, dtype=np.float64)[None, :]
    c = np.sqrt(2.0 / n) * np.cos(np.pi * (x + 0.5) * k / n)
    c[0] *= np.sqrt(0.5)
    return c.astype(np.float32)


def folded_bases():
    cx, cy = basis64(GX), basis64(GY)
    order = np.arange(GX).reshape(GX // FOLD, FOLD).T.reshape(-1)
    cxp = cx[order][:, order]
    return [np.ascontiguousarray(a).astype(ml_dtypes.bfloat16) for a in (cxp, cxp.T, cy, cy.T)]


def mm(a, b):
    return jnp.dot(a, b, preferred_element_type=F32)


def unfold(wide):
    return jnp.concatenate([wide[:, r * GY : (r + 1) * GY] for r in range(FOLD)], axis=0)


def fold(tall):
    q = GX // FOLD
    return jnp.concatenate([tall[r * q : (r + 1) * q] for r in range(FOLD)], axis=1)


def xor_of(bits, k):
    return sum(lax.rem(b + lax.rem(lax.div(k, 1 << i), 2), 2) * (1 << i) for i, b in enumerate(bits))


def gather_lanes(rows, lanes):
    return jnp.take_along_axis(rows, lanes, axis=1, mode="promise_in_bounds")


def step_kernel(nt, ns, n_in, *refs):
    sources, (out, cost_out), held = refs[:n_in], refs[n_in : n_in + 2], refs[n_in + 2 :]
    landed, in_sem, held = held[:n_in], held[n_in], held[n_in + 1 :]
    control, spectrum, cy, cxpt, index, perturb, innov, sigma, qc, cxp, cyt = landed
    (
    flat, send_f, recv_f, spread, table, hi_hot, lo_hot, upd, prod,
    send_a, recv_a, part, parts, sf_sem, rf_sem, sa_sem, ra_sem, sp_sem, rp_sem,
    ) = held
    n = nt * ns
    my_t, my_s = lax.axis_index("tm"), lax.axis_index("space")
    me = my_t * ns + my_s
    slots, levels, piece = sources[5].shape[0], sources[5].shape[2], sources[5].shape[3]
    rows = piece // LANES
    cells = rows * levels
    sent = rows + rows % 2
    pad_rows = send_f.shape[1]
    q, width = GX // FOLD, FOLD * GY
    tiles = width // LANES
    chunks = index.shape[0] // slots
    group = 8
    bits = [lax.rem(lax.div(me, 1 << i), 2) for i in range(n.bit_length() - 1)]
    n_groups = n // group
    cuts = (20, 14, 0) if rows > 20 else (0,)
    ends = (rows,) + cuts[:-1]
    ranges = [(a, b - a, b - a + (b - a) % 2) for a, b in zip(cuts, ends)]

    def device(peer):
        return (lax.div(peer, ns), lax.rem(peer, ns))

    def peer_of(k):
        return me + sum((1 - 2 * b) * (1 << i) for i, b in enumerate(bits) if k >> i & 1)

    def load(i):
        return pltpu.make_async_copy(sources[i], landed[i], in_sem.at[i])

    for i in (0, 1, 2, 3):
        load(i).start()

    barrier = pltpu.get_barrier_semaphore()

    for k in range(n - 1, 0, -1):
        pl.semaphore_signal(
            barrier, inc=1, device_id=device(peer_of(k)), device_id_type=MESH_ID
        )
    load(4).start()

    def wide_of(ref):
        return jnp.concatenate(
            [ref[pl.ds(a, q, stride=tiles), :] for a in range(tiles)], axis=1
        )

    def flat_from(wide):
        for a in range(tiles):
            flat[pl.ds(a, q, stride=tiles), :] = wide[:, a * LANES : (a + 1) * LANES]

    for i in (0, 1, 2):
        load(i).wait()
    ctl = wide_of(control)
    spec = wide_of(spectrum)
    mid = mm(unfold((ctl * spec).astype(BF16)), cy[...]).astype(BF16)
    load(3).wait()
    flat_from(fold(mm(cxpt[...], mid)))
    flat[q * tiles :, :] = jnp.zeros((flat.shape[0] - q * tiles, LANES), F32)
    for s in range(ns):
        send_f[s] = flat[s * rows : s * rows + pad_rows, :].astype(BF16)

    pl.semaphore_wait(barrier, n - 1)

    def f_copy(p, k):
        peer = peer_of(k)
        t, s = device(peer)
        at = pl.ds(ranges[p][0], ranges[p][2])
        return pltpu.make_async_remote_copy(
            send_f.at[s, at], recv_f.at[me, at], sf_sem, rf_sem.at[p * n_groups + k // group],
            device_id=(t, s), device_id_type=MESH_ID,
        )

    for p in range(len(ranges)):
        for k in range(n - 1, 0, -1):
            f_copy(p, k).start()
    recv_f[me] = send_f[my_s]

    for j in range(rows):
        pltpu.make_async_copy(
            sources[5].at[:, :, :, pl.ds(j * LANES, LANES)],
            perturb.at[:, :, pl.ds(j * levels, levels), :], in_sem.at[5],
        ).start()
    for i in range(6, n_in):
        load(i).start()

    back = 0.5 * jnp.sum(ctl * ctl, axis=0, keepdims=True)
    back = sum(back[:, a * LANES : (a + 1) * LANES] for a in range(tiles))
    table[...] = jnp.zeros(table.shape, F32)
    send_a[...] = jnp.zeros(send_a.shape, BF16)
    load(4).wait()
    hi_rows, lo_cols = hi_hot.shape[1], lo_hot.shape[2]
    his, los = [], []
    for t in range(slots):
        ix = index[pl.ds(t, chunks, stride=slots), :]
        level, point = ix // piece, ix % piece
        hi, lo = (point // LANES) * levels + level, point % LANES
        his.append(hi)
        los.append(lo)
        col = lo.T
        for c in range(chunks):
            at = pl.ds(c * LANES, LANES)
            hi_hot[t, :, at] = jnp.where(
                lax.broadcasted_iota(jnp.int32, (hi_rows, LANES), 0) == hi[c : c + 1, :], 1.0, 0.0
            ).astype(BF16)
            lo_hot[t, at, :] = jnp.where(
                lax.broadcasted_iota(jnp.int32, (LANES, lo_cols), 1) == col[:, c : c + 1], 1.0, 0.0
            ).astype(BF16)
    whole = perturb.at[:, :, pl.ds(0, cells), :]
    pltpu.make_async_copy(whole, whole, in_sem.at[5]).wait()

    block_bits = bits[group.bit_length() - 1 :]

    for i in (6, 7, 8):
        load(i).wait()
    models = [jnp.zeros((chunks, LANES), F32) for t in range(slots)]
    known = []
    for t in range(slots):
        mine = pl.ds(t, chunks, stride=slots)
        qct = qc[mine, :]
        rad = jnp.where(qct == 0, 4.0, jnp.where(qct == 1, 2.0, 1.0)).astype(F32)
        known.append((rad, 1.0 / (rad * rad), innov[mine, :], 1.0 / sigma[mine, :]))

    def add_group(p, g, own):
        r0, real, wide = ranges[p]
        at = pl.ds(r0 * levels, real * levels)
        block = xor_of(block_bits, g)
        arrived = recv_f.at[pl.ds(0, group - own), pl.ds(0, wide)]
        pltpu.make_async_copy(arrived, arrived, rf_sem.at[p * n_groups + g]).wait()
        for i in range(group):
            f = recv_f[block * group + i, r0:, :].astype(F32)[:real]
            for l in range(levels):
                spread[i, pl.ds(r0 * levels + l, real, stride=levels), :] = f
        for t in range(slots):
            total = table[t, at, :]
            for i in range(group):
                v = perturb[t, block * group + i, at, :].astype(F32)
                total = total + v * spread[i, at, :]
            table[t, at, :] = total

    def increments(p):
        add_group(p, 0, 1)

        def next_group(i, c):
            g = lax.rem(2 * i, n_groups) + lax.div(2 * i, n_groups)
            add_group(p, g, 0)
            return c

        lax.fori_loop(1, n_groups, next_group, 0)

    costs = [None] * slots

    def observe(p):
        r0, real, wide = ranges[p]
        top = hi_rows if r0 + real == rows else (r0 + real) * levels
        for t in range(slots):
            for h in range(r0 * levels, (r0 + real) * levels):
                picked = gather_lanes(
                    jnp.broadcast_to(table[t, h : h + 1, :], (chunks, LANES)), los[t]
                )
                models[t] = jnp.where(his[t] == h, picked, models[t])
            rad, bent, seen, inv = known[t]
            scaled = (models[t] - seen) * inv
            sq = scaled * scaled * bent
            costs[t] = (rad, sq)
            g = scaled * inv / (1.0 + sq)
            terms = jnp.concatenate(
                [
                    hi_hot[t, r0 * levels : top, c * LANES : (c + 1) * LANES]
                    * jnp.broadcast_to(g[c : c + 1, :], (top - r0 * levels, LANES)).astype(BF16)
                    for c in range(chunks)
                ],
                axis=1,
            )
            upd[t, r0 * levels : top, :] = mm(terms, lo_hot[t]).astype(BF16).astype(F32)

    def a_copy(p, peer, far):
        at = pl.ds(ranges[p][0], ranges[p][2])
        return pltpu.make_async_remote_copy(
            send_a.at[peer, at], recv_a.at[me, at], sa_sem, ra_sem.at[far],
            device_id=device(peer), device_id_type=MESH_ID,
        )

    def one_member(p, m, i, to):
        r0, real, wide = ranges[p]
        at = pl.ds(r0 * levels, real * levels)
        prod[i, at, :] = sum(
            perturb[t, m, at, :].astype(F32) * upd[t, at, :] for t in range(slots)
        )
        to[pl.ds(r0, real), :] = sum(
            prod[i, pl.ds(r0 * levels + l, real, stride=levels), :] for l in range(levels)
        ).astype(BF16)

    def low_of(i):
        return sum((1 - 2 * b) * (1 << j) for j, b in enumerate(bits[:3]) if i >> j & 1)

    def adjoints(p):
        def eight(d, c):
            base = xor_of(block_bits, n_groups - 1 - d) * group + lax.rem(me, group)
            peers = [base + low_of(i) for i in range(group - 1, -1, -1)]
            for i, peer in enumerate(peers):
                one_member(p, peer, i, send_a.at[peer])
            for peer in peers:
                a_copy(p, peer, lax.rem(n_groups - 1 - d, 2)).start()
            return c

        lax.fori_loop(0, n_groups - 1, eight, 0)
        peers = [peer_of(i) for i in range(group - 1, 0, -1)]
        for i, peer in enumerate(peers):
            one_member(p, peer, i, send_a.at[peer])
        one_member(p, me, group - 1, recv_a.at[me])
        for peer in peers:
            a_copy(p, peer, 0).start()

    for p in range(len(ranges)):
        increments(p)
        observe(p)
        adjoints(p)

    cost_row = back
    for rad, sq in costs:
        cost_row = cost_row + jnp.sum(0.5 * rad * rad * jnp.log1p(sq), axis=0, keepdims=True)
    part[0:1, :] = cost_row
    for i in (9, 10):
        load(i).wait()

    for far in (0, 1):
        pieces = n // 2 - 1 + far
        arrived = recv_a.at[pl.ds(0, pieces), pl.ds(0, sent)]
        pltpu.make_async_copy(arrived, arrived, ra_sem.at[far]).wait()
        half = lax.rem(block_bits[0] + far, 2)
        for i in range(ns // 2):
            s = half * (ns // 2) + i
            at = pl.multiple_of(half * (ns // 2 * rows), 8) + i * rows
            flat[pl.ds(at, rows), :] = sum(
                recv_a[t * ns + s].astype(F32)[:rows] for t in range(nt)
            )
    mid = mm(cxp[...], unfold(wide_of(flat).astype(BF16))).astype(BF16)
    gr = ctl + spec * fold(mm(mid, cyt[...]))
    sq = jnp.sum(gr * gr, axis=0, keepdims=True)
    part[1:2, :] = sum(sq[:, a * LANES : (a + 1) * LANES] for a in range(tiles))

    def s_copy(k):
        peer = peer_of(k)
        return pltpu.make_async_remote_copy(
            part, parts.at[me], sp_sem, rp_sem, device_id=device(peer), device_id_type=MESH_ID,
        )

    for k in range(n - 1, 0, -1):
        s_copy(k).start()
    parts[me] = part[...]
    flat_from(gr)
    all_sent = send_a.at[pl.ds(0, n - 1), pl.ds(0, sent)]
    pltpu.make_async_copy(all_sent, all_sent, sf_sem).wait()
    pltpu.make_async_copy(all_sent, all_sent, sa_sem).wait()

    all_parts = parts.at[pl.ds(0, n - 1)]
    pltpu.make_async_copy(all_parts, all_parts, sp_sem).wait()
    pltpu.make_async_copy(all_parts, all_parts, rp_sem).wait()
    sums = [parts[i] for i in range(n)]
    while len(sums) > 1:
        sums = [a + b for a, b in zip(sums[::2], sums[1::2])]
    sums = jnp.sum(sums[0], axis=1, keepdims=True)
    total_cost, grad_sq = sums[0:1, :], sums[1:2, :]
    step = 0.5 * total_cost / (grad_sq + 1e-06)
    out[...] = control[...] - step * flat[: q * tiles, :]
    cost_out[...] = jnp.broadcast_to(total_cost, cost_out.shape)


def put_kernel(out, cost, out_to, cost_to, sem):
    copies = [
        pltpu.make_async_copy(src, dst, sem.at[i])
        for i, (src, dst) in enumerate(((out, out_to), (cost, cost_to)))
    ]
    for copy in copies:
        copy.start()
    for copy in copies:
        copy.wait()


def fused_device(nt, ns, control, spectrum, perturb, obs_index, innovation, obs_sigma, qc_class):
    n = nt * ns
    slots, members, levels, piece = perturb.shape
    grid_rows = GX * GY // LANES
    rows = piece // LANES
    cells = rows * levels
    pad_rows = -(-rows // 16) * 16
    pad_cells = -(-cells // 16) * 16
    hi_rows = pad_cells
    obs = obs_index.shape[1]
    vm = pl.BlockSpec(memory_space=pltpu.VMEM)
    dma = pltpu.SemaphoreType.DMA
    cxp, cxpt, cy, cyt = [jnp.asarray(b) for b in folded_bases()]

    def by_chunk(x):
        return x.reshape(slots, obs // LANES, LANES).transpose(1, 0, 2).reshape(-1, LANES)

    sources = [
        control.reshape(grid_rows, LANES), spectrum.reshape(grid_rows, LANES), cy, cxpt,
        by_chunk(obs_index), perturb, by_chunk(innovation), by_chunk(obs_sigma),
        by_chunk(qc_class), cxp, cyt,
    ]
    lands = [pltpu.VMEM(a.shape, a.dtype) for a in sources]
    lands[5] = pltpu.VMEM((slots, members, pad_cells, LANES), BF16)
    out, cost = pl.pallas_call(
        functools.partial(step_kernel, nt, ns, len(sources)),
        out_shape=(
            jax.ShapeDtypeStruct((grid_rows, LANES), F32),
            jax.ShapeDtypeStruct((1, LANES), F32),
        ),
        in_specs=[pl.BlockSpec(memory_space=pltpu.HBM)] * len(sources),
        out_specs=(vm, vm),
        scratch_shapes=[
            *lands,
            dma((len(sources),)),
            pltpu.VMEM((grid_rows + 16, LANES), F32),
            pltpu.VMEM((ns, pad_rows, LANES), BF16),
            pltpu.VMEM((n, pad_rows, LANES), BF16),
            pltpu.VMEM((8, pad_cells, LANES), F32),
            pltpu.VMEM((slots, pad_cells, LANES), F32),
            pltpu.VMEM((slots, hi_rows, obs), BF16),
            pltpu.VMEM((slots, obs, LANES), BF16),
            pltpu.VMEM((slots, pad_cells, LANES), F32),
            pltpu.VMEM((8, pad_cells, LANES), F32),
            pltpu.VMEM((n, pad_rows, LANES), BF16),
            pltpu.VMEM((n, pad_rows, LANES), BF16),
            pltpu.VMEM((2, LANES), F32),
            pltpu.VMEM((n, 2, LANES), F32),
            dma, dma((3 * n // 8,)), dma, dma((2,)), dma, dma,
        ],
        compiler_params=pltpu.CompilerParams(
            collective_id=0, has_side_effects=True, vmem_limit_bytes=24 << 20
        ),
        name="envar_step",
    )(*[pltpu.with_memory_space_constraint(a, pltpu.HBM) for a in sources])
    out, cost = pl.pallas_call(
        put_kernel,
        out_shape=(
            jax.ShapeDtypeStruct((grid_rows, LANES), F32),
            jax.ShapeDtypeStruct((1, LANES), F32),
        ),
        in_specs=[pl.BlockSpec(memory_space=pltpu.VMEM)] * 2,
        out_specs=[pl.BlockSpec(memory_space=pltpu.HBM)] * 2,
        scratch_shapes=[dma((2,))],
        name="put_results",
    )(*[pltpu.with_memory_space_constraint(a, pltpu.VMEM) for a in (out, cost)])
    return out.reshape(control.shape), cost[0, :1]


def fused_fits(nt, ns, control, perturb, innovation):
    n = nt * ns
    piece = GX * GY // ns
    return (
        nt == 2
        and ns == 16
        and control.shape[0] == n
        and perturb.shape[2] == 4
        and piece % LANES == 0
        and (FOLD * GY) % LANES == 0
        and (GX // FOLD) % 8 == 0
        and innovation.shape[1] // ns == 16 * LANES
    )


def solution(mesh):
    nt, ns = mesh.shape["tm"], mesh.shape["space"]

    def whole(control, spectrum, perturb, obs_index, innovation, obs_sigma, qc_class):
        fits = fused_fits(nt, ns, control, perturb, innovation)
        body = functools.partial(fused_device, nt, ns) if fits else per_device
        return on_mesh(mesh, body)(
            control, spectrum, perturb, obs_index, innovation, obs_sigma, qc_class
        )

    return whole


def on_mesh(mesh, body):
    in_specs = (
        P(("tm", "space"), None),
        P(),
        P("tm", None, None, "space"),
        P("tm", "space"),
        P("tm", "space"),
        P("tm", "space"),
        P("tm", "space"),
    )
    out_specs = (P(("tm", "space"), None), P())
    return jax.shard_map(
        body, mesh=mesh, in_specs=in_specs, out_specs=out_specs, check_vma=False
    )
```
